32 devices in a mesh: face: 8 (over y, x, core), member: 4 (over z).
Axes of the slice: x: 2, y: 2, z: 4, core: 2. Of those that a mesh axis runs over, the one named last changes fastest.
Arguments:
- features: bfloat16 [8, 48, 16, 16, 256], P('member', 'face'), may hold values from -6 to 6
- observed: bfloat16 [48, 80, 256], P('face', None, 'member'), may hold values from -6 to 6
- conv_weights: bfloat16 [2304, 2, 256], P(('face', 'member')), may hold values from -0.125 to 0.125
- head_weight: bfloat16 [256, 80], P(('face', 'member')), may hold values from -0.375 to 0.375
- adjacency: int32 [48, 4, 3], replicated, may hold values from 0 to 47, as said below
- placement_map: int32 [48], replicated, may hold values from 0 to 47, each once
Outputs:
- conv_grads: float32 [2304, 2, 256], P(('face', 'member'))
- head_grad: float32 [256, 80], P(('face', 'member'))
The draws below stay inside these ranges and needn't reach their ends.
Inputs may be any that keep to these rules, and one draw needn't show every extreme that they name: `adjacency`: the table is the gluing of the 12 HEALPix base faces, each cut into 4 square tiles, under a labelling of the tiles drawn from the seed: entry [t, a] = (n, b, f) glues side a of tile t to side b of tile n, reversed when f is 1; the gluing is mutual (entry [n, b] is (t, a, f)) and never joins a side to itself. `placement_map`: each tile stands at exactly one slot.
All inputs are finite; a program needn't handle non-finite values.
Results may differ from the reference program's by a relative error of at most 0.0005.
Values may be sent and summed in bfloat16 or wider, within the bound.
A program may use at most 128 MiB of HBM per device.

```python
import math
import jax
import jax.numpy as jnp
import numpy as np
from jax import lax

C = 256
VARS = 80
FACES = 12
TILES_FACE = 4
TILE = 16
MEMBERS = 8
TILE_TOTAL = 48


def face_gluing(face, side):
    cycle, pos = divmod(face, 4)
    if cycle == 0:
        table = [((pos - 1) % 4, 1, 1), ((pos + 1) % 4, 0, 1), (4 + (pos + 1) % 4, 0, 0), (4 + pos, 1, 0)]
    elif cycle == 1:
        table = [((pos - 1) % 4, 2, 0), (pos, 3, 0), (8 + pos, 0, 0), (8 + (pos - 1) % 4, 1, 0)]
    else:
        table = [(4 + pos, 2, 0), (4 + (pos + 1) % 4, 3, 0), (8 + (pos + 1) % 4, 3, 1), (8 + (pos - 1) % 4, 2, 1)]
    return table[side]


def tile_on_side(side, place, width):
    if side == 0:
        return (0, place)
    if side == 1:
        return (place, width - 1)
    if side == 2:
        return (width - 1, place)
    return (place, 0)


def canonical_table():
    width = math.isqrt(TILES_FACE)
    rows_out = []
    for face in range(FACES):
        for tile_row in range(width):
            for tile_col in range(width):
                base = face * width * width
                entry = []
                for side in range(4):
                    inside = [tile_row > 0, tile_col < width - 1, tile_row < width - 1, tile_col > 0][side]
                    if inside:
                        step_row = [-1, 0, 1, 0][side]
                        step_col = [0, 1, 0, -1][side]
                        entry.append([base + (tile_row + step_row) * width + tile_col + step_col, (side + 2) % 4, 0])
                    else:
                        place = tile_col if side in (0, 2) else tile_row
                        other_face, other_side, flip_bit = face_gluing(face, side)
                        if flip_bit == 1:
                            place = width - 1 - place
                        other_row, other_col = tile_on_side(other_side, place, width)
                        entry.append([other_face * width * width + other_row * width + other_col, other_side, flip_bit])
                rows_out.append(entry)
    return np.array(rows_out, dtype=np.int32)


def draw_adjacency(key, part):
    canonical_order = jnp.asarray(canonical_table())
    label_list = jax.random.permutation(jax.random.fold_in(key, 11), TILE_TOTAL).astype(jnp.int32)
    renumbered_labels = jnp.stack([label_list[canonical_order[:, :, 0]], canonical_order[:, :, 1], canonical_order[:, :, 2]], axis=-1).astype(jnp.int32)
    return jnp.zeros((TILE_TOTAL, 4, 3), jnp.int32).at[label_list].set(renumbered_labels)


def with_spikes(values, stream_key, source, target, shards_of, factor):
    owner, partner = [(jnp.arange(values.shape[axis_at]) // (values.shape[axis_at] // shards_of)).reshape([-1 if axis == axis_at else 1 for axis in range(values.ndim)]) for axis_at in (source, target)]
    chosen = jax.random.permutation(stream_key, shards_of)[partner]
    strong = (owner == chosen) | (owner == (partner + shards_of // 2) % shards_of)
    return jnp.where(strong, factor * values, values)


def levels(own_key, shape, pieces, least, largest):
    factor_of = 1.0
    for dim, parts in pieces:
        heights = jax.random.uniform(jax.random.fold_in(jax.random.fold_in(own_key, 6), dim), (parts,), jnp.float32, least / len(pieces), largest / len(pieces))
        factor_of = factor_of * jnp.repeat(jnp.exp(heights), shape[dim] // parts).reshape((-1,) + (1,) * (len(shape) - 1 - dim))
    return factor_of


def bell_draw(rng, extent, scale, reach, pieces=(), held_as=jnp.bfloat16):
    values = scale * jax.random.normal(rng, extent, jnp.float32)
    if pieces:
        values = values * levels(rng, extent, pieces, -0.22, 0.18)
    return jnp.clip(values, -reach, reach).astype(held_as)


def heavy_noise(own_key, dims, deviation, most, shards, heavy, kind=jnp.bfloat16):
    values = deviation * jax.random.normal(own_key, dims, jnp.float32)
    if shards:
        values = values * levels(own_key, dims, shards, -0.22, 0.18)
    return jnp.clip(with_spikes(values, jax.random.fold_in(own_key, 3), *heavy), -most, most).astype(kind)


def setup_inputs(seed: int = 0) -> dict:
    splits = jax.random.split(jax.random.key(seed), 7)
    features = heavy_noise(splits[0], (MEMBERS, TILE_TOTAL, TILE, TILE, C), 1.0, 6.0, ((0, 4), (1, 8)), (1, 4, 8, 2.0))
    observed = bell_draw(splits[1], (TILE_TOTAL, VARS, TILE * TILE), 1.0, 6.0, ((0, 8), (2, 4)))
    conv_weights = bell_draw(splits[2], (9 * C, 2, C), (9 * C) ** -0.5, 0.125, ((0, 32),))
    head_weight = bell_draw(splits[3], (C, VARS), C ** -0.5, 0.375, ((0, 32),))
    adjacency = draw_adjacency(jax.random.fold_in(splits[6], 71), 0)
    placement_map = jax.random.permutation(splits[5], TILE_TOTAL).astype(jnp.int32)
    return {"features": features, "observed": observed, "conv_weights": conv_weights, "head_weight": head_weight, "adjacency": adjacency, "placement_map": placement_map}


smooth_sq = 0.0625

def split_edges(grid_field):
    return jnp.stack([grid_field[:, :, 0], grid_field[:, :, :, -1], grid_field[:, :, -1], grid_field[:, :, :, 0]], axis=2)

def border_of(padded):
    return jnp.stack([padded[:, :, 0, 1:-1], padded[:, :, 1:-1, -1], padded[:, :, -1, 1:-1], padded[:, :, 1:-1, 0]], axis=2)

def surround(grid_field, border):
    ensemble_members, tile_count, height, tile_w, channels = grid_field.shape
    corner = jnp.zeros((ensemble_members, tile_count, 1, 1, channels), grid_field.dtype)
    top_row = jnp.concatenate([corner, border[:, :, 0][:, :, None], corner], axis=3)
    low_row = jnp.concatenate([corner, border[:, :, 2][:, :, None], corner], axis=3)
    middle = jnp.concatenate([border[:, :, 3][:, :, :, None], grid_field, border[:, :, 1][:, :, :, None]], axis=3)
    return jnp.concatenate([top_row, middle, low_row], axis=2)

def convolve(padded, weight):
    channels = weight.shape[1]
    height = padded.shape[2] - 2
    tile_w = padded.shape[3] - 2
    summed = None
    for tap_index in range(9):
        row_off, col_off = divmod(tap_index, 3)
        window = padded[:, :, row_off:row_off + height, col_off:col_off + tile_w, :]
        product_part = jnp.dot(window.reshape(-1, channels), weight[tap_index * channels:(tap_index + 1) * channels], preferred_element_type=jnp.float32)
        summed = product_part if summed is None else summed + product_part
    return summed.reshape(padded.shape[:2] + (height, tile_w, channels))

def transpose_conv(slope_in, weight):
    channels = weight.shape[1]
    ensemble_members, tile_count, height, tile_w, _ = slope_in.shape
    result = jnp.zeros((ensemble_members, tile_count, height + 2, tile_w + 2, channels), jnp.float32)
    flat_slope = slope_in.reshape(-1, channels)
    for tap_index in range(9):
        row_off, col_off = divmod(tap_index, 3)
        product_part = lax.dot_general(flat_slope, weight[tap_index * channels:(tap_index + 1) * channels], (((1,), (1,)), ((), ())), preferred_element_type=jnp.float32)
        result = result.at[:, :, row_off:row_off + height, col_off:col_off + tile_w, :].add(product_part.reshape(slope_in.shape))
    return result

def weight_slope(padded, slope_in):
    channels = slope_in.shape[-1]
    height = slope_in.shape[2]
    tile_w = slope_in.shape[3]
    flat_slope = slope_in.reshape(-1, channels)
    pieces_out = []
    for tap_index in range(9):
        row_off, col_off = divmod(tap_index, 3)
        window = padded[:, :, row_off:row_off + height, col_off:col_off + tile_w, :]
        pieces_out.append(lax.dot_general(window.reshape(-1, channels), flat_slope, (((0,), (0,)), ((), ())), preferred_element_type=jnp.float32))
    return jnp.concatenate(pieces_out, axis=0)

def dsilu(argument):
    sigmoid_v = jax.nn.sigmoid(argument)
    return sigmoid_v * (1.0 + argument * (1.0 - sigmoid_v))

def reference(features, observed, conv_weights, head_weight, adjacency, placement_map):
    ensemble_members, tile_count, height, tile_w, channels = features.shape
    slot_ids = jnp.arange(tile_count, dtype=jnp.int32)
    slot_of = lax.optimization_barrier(jnp.sum(slot_ids[:, None] * (placement_map[:, None] == slot_ids[None, :]).astype(jnp.int32), axis=0))
    entries = adjacency[placement_map]
    source_slot = slot_of[entries[:, :, 0]]
    source_side = entries[:, :, 1]
    flip_flags = entries[:, :, 2]

    def partner_borders(edges):
        picked = edges[:, source_slot, source_side]
        return jnp.where(flip_flags[None, :, :, None, None] == 1, picked[:, :, :, ::-1, :], picked)
    pad_in = surround(features, partner_borders(split_edges(features)))
    pre_one = convolve(pad_in, conv_weights[:, 0, :])
    act_one = jax.nn.silu(pre_one).astype(jnp.bfloat16)
    pad_mid = surround(act_one, partner_borders(split_edges(act_one)))
    pre_two = convolve(pad_mid, conv_weights[:, 1, :])
    act_two = jax.nn.silu(pre_two).astype(jnp.bfloat16)
    flat_two = act_two.reshape(ensemble_members, tile_count, height * tile_w, channels).astype(jnp.float32)
    outputs = jnp.einsum('mtpc,cv->mtvp', flat_two, head_weight.astype(jnp.float32)).astype(jnp.bfloat16)
    out_vals = outputs.astype(jnp.float32)
    obs_vals = observed.astype(jnp.float32)
    paired = jnp.zeros(out_vals.shape, jnp.float32)
    for column_j in range(ensemble_members):
        spread = out_vals - out_vals[column_j]
        paired = paired + spread * lax.rsqrt(spread * spread + smooth_sq)
    own_gap = out_vals - obs_vals[None]
    slope_out = ((own_gap * lax.rsqrt(own_gap * own_gap + smooth_sq) / ensemble_members - paired / (ensemble_members * ensemble_members)) / TILE).astype(jnp.bfloat16)
    slope_f = slope_out.astype(jnp.float32)
    head_grad = jnp.einsum('mtpc,mtvp->cv', flat_two, slope_f)
    back_two = jnp.einsum('mtvp,cv->mtpc', slope_f, head_weight.astype(jnp.float32)).reshape(ensemble_members, tile_count, height, tile_w, channels)
    slope_two = (back_two * dsilu(pre_two)).astype(jnp.bfloat16)
    grad_two = weight_slope(pad_mid, slope_two)
    pad_slope = transpose_conv(slope_two, conv_weights[:, 1, :]).astype(jnp.bfloat16)
    returned = partner_borders(border_of(pad_slope)).astype(jnp.float32)
    slope_mid = pad_slope[:, :, 1:-1, 1:-1].astype(jnp.float32)
    slope_mid = slope_mid.at[:, :, 0].add(returned[:, :, 0])
    slope_mid = slope_mid.at[:, :, :, -1].add(returned[:, :, 1])
    slope_mid = slope_mid.at[:, :, -1].add(returned[:, :, 2])
    slope_mid = slope_mid.at[:, :, :, 0].add(returned[:, :, 3])
    slope_one = (slope_mid * dsilu(pre_one)).astype(jnp.bfloat16)
    grad_one = weight_slope(pad_in, slope_one)
    return (jnp.stack([grad_one, grad_two], axis=1), head_grad)
```

```python
import functools

import jax
import jax.numpy as jnp
from jax import lax
from jax.experimental import pallas as pl
from jax.experimental.pallas import tpu as pltpu
from jax.sharding import PartitionSpec as P

smooth_sq = 0.0625
MESH = pl.DeviceIdType.MESH
VMEM = pltpu.VMEM
f32 = jnp.float32
bf16 = jnp.bfloat16
LIMIT = 60 * 1024 * 1024
NT = (((1,), (1,)), ((), ()))
TN = (((0,), (0,)), ((), ()))
NN = (((1,), (0,)), ((), ()))


def mm(a, b, dims=NN):
    return lax.dot_general(a, b, dims, preferred_element_type=f32)


def rcopy(src, dst, send, recv, **where):
    return pltpu.make_async_remote_copy(
        src_ref=src, dst_ref=dst, send_sem=send, recv_sem=recv, device_id=where, device_id_type=MESH
    )


def greet(chips, members, face_axis, member_axis):
    face = lax.axis_index("face")
    member = lax.axis_index("member")
    core = face % 2
    chip = face // 2
    barrier = pltpu.get_barrier_semaphore()
    count = 0
    if face_axis:
        pl.semaphore_signal(
            barrier, inc=1, device_id={"face": chip * 2 + 1 - core}, device_id_type=MESH
        )
        for j in range(1, chips):
            pl.semaphore_signal(
                barrier,
                inc=1,
                device_id={"face": ((chip + j) % chips) * 2 + core},
                device_id_type=MESH,
            )
        count += chips
    if member_axis:
        for j in range(1, members):
            pl.semaphore_signal(
                barrier, inc=1, device_id={"member": (member + j) % members}, device_id_type=MESH
            )
        count += members - 1
    pl.semaphore_wait(barrier, count)


def line_gather(x_ref, out_at, member, members, sems):
    ups, upr, dns, dnr = sems
    steps = members - 1

    def up(s):
        b = jnp.maximum(member - s, 0)
        return rcopy(
            x_ref if s == 0 else out_at(b),
            out_at(b),
            ups.at[s],
            upr.at[s],
            member=jnp.minimum(member + 1, members - 1),
        )

    def down(s):
        b = jnp.minimum(member + s, members - 1)
        return rcopy(
            x_ref if s == 0 else out_at(b),
            out_at(b),
            dns.at[s],
            dnr.at[s],
            member=jnp.maximum(member - 1, 0),
        )

    def up_goes(s):
        return jnp.logical_and(member - s >= 0, member < members - 1)

    def down_goes(s):
        return jnp.logical_and(member + s < members, member > 0)

    pl.when(up_goes(0))(lambda: up(0).start())
    pl.when(down_goes(0))(lambda: down(0).start())
    for s in range(steps):
        pl.when(member - 1 - s >= 0)(lambda: up(s).wait_recv())
        if s + 1 < steps:
            pl.when(up_goes(s + 1))(lambda: up(s + 1).start())
        pl.when(member + 1 + s < members)(lambda: down(s).wait_recv())
        if s + 1 < steps:
            pl.when(down_goes(s + 1))(lambda: down(s + 1).start())
    for s in range(steps):
        pl.when(up_goes(s))(lambda: up(s).wait_send())
        pl.when(down_goes(s))(lambda: down(s).wait_send())


class FaceGather:
    def __init__(self, src, out, chips, sems):
        self.src, self.out, self.chips = src, out, chips
        self.send, self.recv, self.fsend, self.frecv = sems
        face = lax.axis_index("face")
        self.face, self.core, self.chip = face, face % 2, face // 2
        self.partner = self.chip * 2 + 1 - self.core

    def direct(self, j):
        return rcopy(
            self.src,
            self.out.at[self.face],
            self.send.at[j],
            self.recv.at[j],
            face=((self.chip + j) % self.chips) * 2 + self.core,
        )

    def forward(self, j):
        block = ((self.chip + self.chips - j) % self.chips) * 2 + self.core
        return rcopy(
            self.src if j == 0 else self.out.at[block],
            self.out.at[block],
            self.fsend.at[j],
            self.frecv.at[j],
            face=self.partner,
        )

    def start(self):
        for j in range(1, self.chips):
            self.direct(j).start()
        self.forward(0).start()

    def relay(self):
        for j in range(1, self.chips):
            self.direct(j).wait_recv()
            self.forward(j).start()

    def finish(self):
        for j in range(1, self.chips):
            self.direct(j).wait_send()
        for j in range(self.chips):
            self.forward(j).wait()


def dma_sems(*sizes):
    return [pltpu.SemaphoreType.DMA((max(n, 1),)) for n in sizes]


def first_gather_kernel(chips, members, count, *refs):
    edges, ws = refs[0], refs[1 : 1 + count]
    edges_out, outs = refs[1 + count], refs[2 + count : 2 + 2 * count]
    sems = refs[2 + 2 * count :]
    own_sem, sems = sems[0], sems[1:]
    face = lax.axis_index("face")
    member = lax.axis_index("member")
    own = [pltpu.make_async_copy(edges, edges_out.at[face], own_sem.at[0])]
    for k in range(count):
        own.append(
            pltpu.make_async_copy(ws[k], outs[k].at[face, member], own_sem.at[k + 1])
        )
    for c in own:
        c.start()
    greet(chips, members, True, True)
    eg = FaceGather(edges, edges_out, chips, sems[:4])
    eg.start()
    for c in own:
        c.wait()
    rest = sems[4:]
    wgs = []
    for k in range(count):
        line = rest[8 * k : 8 * k + 4]
        line_gather(ws[k], lambda b: outs[k].at[face, b], member, members, line)
        wg = FaceGather(outs[k].at[face], outs[k], chips, rest[8 * k + 4 : 8 * k + 8])
        wg.start()
        wgs.append(wg)
    eg.relay()
    for wg in wgs:
        wg.relay()
    eg.finish()
    for wg in wgs:
        wg.finish()


def first_gather(edges, ws, faces, members):
    chips = faces // 2
    count = len(ws)
    shapes = [jax.ShapeDtypeStruct((faces,) + edges.shape, edges.dtype)] + [
        jax.ShapeDtypeStruct((faces, members) + w.shape, w.dtype) for w in ws
    ]
    sems = dma_sems(count + 1) + dma_sems(*([chips] * 4))
    for _ in ws:
        sems += dma_sems(*([members] * 4)) + dma_sems(*([chips] * 4))
    return pl.pallas_call(
        functools.partial(first_gather_kernel, chips, members, count),
        out_shape=shapes,
        in_specs=[pl.BlockSpec(memory_space=VMEM)] * (count + 1),
        out_specs=[pl.BlockSpec(memory_space=VMEM)] * (count + 1),
        scratch_shapes=sems,
        compiler_params=pltpu.CompilerParams(
            collective_id=1, has_side_effects=True, vmem_limit_bytes=LIMIT
        ),
        name="first_gather",
    )(edges, *ws)


def face_gather_kernel(chips, x, out, own_sem, *sems):
    own = pltpu.make_async_copy(x, out.at[lax.axis_index("face")], own_sem.at[0])
    own.start()
    greet(chips, 1, True, False)
    g = FaceGather(x, out, chips, sems)
    g.start()
    own.wait()
    g.relay()
    g.finish()


def face_gather(x, faces, ident):
    chips = faces // 2
    return pl.pallas_call(
        functools.partial(face_gather_kernel, chips),
        out_shape=jax.ShapeDtypeStruct((faces,) + x.shape, x.dtype),
        in_specs=[pl.BlockSpec(memory_space=VMEM)],
        out_specs=pl.BlockSpec(memory_space=VMEM),
        scratch_shapes=dma_sems(1) + dma_sems(*([chips] * 4)),
        compiler_params=pltpu.CompilerParams(
            collective_id=ident, has_side_effects=True, vmem_limit_bytes=LIMIT
        ),
        name="face_gather",
    )(x)


def member_gather_kernel(members, x, out, own_sem, *sems):
    member = lax.axis_index("member")
    own = pltpu.make_async_copy(x, out.at[member], own_sem.at[0])
    own.start()
    greet(1, members, False, True)
    line_gather(x, lambda b: out.at[b], member, members, sems)
    own.wait()


def member_gather(x, members, ident):
    return pl.pallas_call(
        functools.partial(member_gather_kernel, members),
        out_shape=jax.ShapeDtypeStruct((members,) + x.shape, x.dtype),
        in_specs=[pl.BlockSpec(memory_space=VMEM)],
        out_specs=pl.BlockSpec(memory_space=VMEM),
        scratch_shapes=dma_sems(1) + dma_sems(*([members] * 4)),
        compiler_params=pltpu.CompilerParams(
            collective_id=ident, has_side_effects=True, vmem_limit_bytes=LIMIT
        ),
        name="member_gather",
    )(x)


def scatter_kernel(chips, members, count, *refs):
    gs, outs = refs[:count], refs[count : 2 * count]
    scratch = refs[2 * count :]
    face = lax.axis_index("face")
    member = lax.axis_index("member")
    core, chip = face % 2, face // 2
    partner = chip * 2 + 1 - core
    greet(chips, members, True, True)

    def parts(k):
        return scratch[10 * k : 10 * k + 10]

    def there(j):
        return (chip + j) % chips

    def core_copy(k, j):
        fromcore, _, _, _, s0, r0, _, _, _, _ = parts(k)
        return rcopy(
            gs[k].at[there(j), 1 - core], fromcore.at[j], s0.at[j], r0.at[j], face=partner
        )

    def chip_copy(k, j):
        _, acc, fromchip, _, _, _, s1, r1, _, _ = parts(k)
        return rcopy(acc.at[j], fromchip.at[j], s1.at[j], r1.at[j], face=there(j) * 2 + core)

    def line_copy(k, j):
        _, acc, _, fromline, _, _, _, _, s2, r2 = parts(k)
        to = (member + j) % members
        return rcopy(acc.at[0, to], fromline.at[j], s2.at[j], r2.at[j], member=to)

    order = list(range(1, chips)) + [0]
    for k in range(count):
        for j in order:
            core_copy(k, j).start()
    for k in range(count):
        fromcore, acc = parts(k)[:2]
        for j in order:
            core_copy(k, j).wait_recv()
            acc[j] = gs[k][there(j), core] + fromcore[j]
            if j:
                chip_copy(k, j).start()
    for k in range(count):
        acc, fromchip = parts(k)[1:3]
        for j in range(1, chips):
            chip_copy(k, j).wait_recv()
            acc[0] = acc[0] + fromchip[j]
        for j in range(1, members):
            line_copy(k, j).start()
    for k in range(count):
        acc, fromline = parts(k)[1], parts(k)[3]
        total = acc[0, member]
        for j in range(1, members):
            line_copy(k, j).wait_recv()
            total = total + fromline[j]
        outs[k][...] = total
    for k in range(count):
        for j in range(chips):
            core_copy(k, j).wait_send()
        for j in range(1, chips):
            chip_copy(k, j).wait_send()
        for j in range(1, members):
            line_copy(k, j).wait_send()


def scatter(gs, faces, members, ident):
    chips = faces // 2
    scratch = []
    for g in gs:
        tail = g.shape[3:]
        scratch += [
            VMEM((chips, members) + tail, f32),
            VMEM((chips, members) + tail, f32),
            VMEM((chips, members) + tail, f32),
            VMEM((members,) + tail, f32),
        ] + dma_sems(chips, chips, chips, chips, members, members)
    return pl.pallas_call(
        functools.partial(scatter_kernel, chips, members, len(gs)),
        out_shape=[jax.ShapeDtypeStruct(g.shape[3:], f32) for g in gs],
        in_specs=[pl.BlockSpec(memory_space=VMEM)] * len(gs),
        out_specs=[pl.BlockSpec(memory_space=VMEM)] * len(gs),
        scratch_shapes=scratch,
        compiler_params=pltpu.CompilerParams(
            collective_id=ident, has_side_effects=True, vmem_limit_bytes=LIMIT
        ),
        name="scatter",
    )(*gs)


def rims_of(index_ref, flip_ref, edges_ref, n, length):
    cat = jnp.concatenate([edges_ref[index_ref[n * 4 + a]] for a in range(4)], axis=0)
    size = 4 * length
    row = lax.broadcasted_iota(jnp.int32, (size, size), 0)
    col = lax.broadcasted_iota(jnp.int32, (size, size), 1)
    side = row // length
    place = row - side * length
    flag = jnp.zeros((size, size), jnp.int32)
    for a in range(4):
        flag = jnp.where(side == a, flip_ref[n * 4 + a], flag)
    target = side * length + jnp.where(flag == 1, length - 1 - place, place)
    return mm(jnp.where(col == target, 1.0, 0.0).astype(bf16), cat)


def col_to_rows(ref_slice):
    height, _, channels = ref_slice.shape
    return ref_slice.reshape(height, channels)


def sides_out(field, edge_ref, k):
    w = field.shape[1]
    h = field.shape[0]
    edge_ref[k, 0] = field[0].astype(bf16)
    edge_ref[k, 1] = col_to_rows(field[:, w - 1 : w, :]).astype(bf16)
    edge_ref[k, 2] = field[h - 1].astype(bf16)
    edge_ref[k, 3] = col_to_rows(field[:, 0:1, :]).astype(bf16)


def silu(v):
    return v / (1.0 + jnp.exp(-v))


def dsilu(v):
    s = 1.0 / (1.0 + jnp.exp(-v))
    return s * (1.0 + v * (1.0 - s))


def conv_kernel(block, last, *refs):
    index_ref, flip_ref, x_ref, edges_ref, w_ref = refs[:5]
    if last:
        head_ref, x3_ref, pre_ref, act_ref, out_ref, pad = refs[5:]
    else:
        x3_ref, pre_ref, act_ref, side_ref, pad, field = refs[5:]
    _, h, w, c = x_ref.shape
    step = pl.program_id(0)
    for k in range(block):
        n = step * block + k
        rims = rims_of(index_ref, flip_ref, edges_ref, n, w)
        zero = jnp.zeros((8, c), f32)
        for r in (0, h + 1):
            pad[r, 0:8, :] = zero
            pad[r, 8 + w : 16 + w, :] = zero
        pad[1 : h + 1, 8 : 8 + w, :] = x_ref[k].astype(f32)
        pad[0, 8 : 8 + w, :] = rims[0:w]
        pad[1 : h + 1, 8 + w : 9 + w, :] = rims[w : w + h].reshape(h, 1, c)
        pad[h + 1, 8 : 8 + w, :] = rims[w + h : 2 * w + h]
        pad[1 : h + 1, 7:8, :] = rims[2 * w + h :].reshape(h, 1, c)
        for b in range(3):
            x3_ref[k, :, :, b * c : (b + 1) * c] = pad[:, 7 + b : 7 + b + w, :].astype(bf16)
    pre = None
    for a in range(3):
        part = mm(
            x3_ref[:, a : a + h].reshape(block * h * w, 3 * c),
            w_ref[3 * a * c : 3 * (a + 1) * c, :],
        )
        pre = part if pre is None else pre + part
    pre_ref[...] = pre.reshape(block, h * w, c)
    act = silu(pre).astype(bf16)
    act_ref[...] = act.reshape(act_ref.shape)
    if last:
        for k in range(block):
            out_ref[k] = mm(head_ref[...], act[k * h * w : (k + 1) * h * w], NT).astype(bf16)
    else:
        for k in range(block):
            field[...] = act[k * h * w : (k + 1) * h * w].astype(f32).reshape(h, w, c)
            sides_out(field, side_ref, k)


def whole(shape):
    return pl.BlockSpec(shape, lambda i: (0,) * len(shape))


def tiles(block, shape):
    return pl.BlockSpec((block,) + shape, lambda i: (i,) + (0,) * len(shape))


SMEM_SPEC = pl.BlockSpec(memory_space=pltpu.SMEM)


def block_of(n):
    return 3 if n % 3 == 0 else (2 if n % 2 == 0 else 1)


def conv(index, flips, x, edges, w, head_t=None):
    n, h, wd, c = x.shape
    block = block_of(n)
    last = head_t is not None
    in_specs = [
        SMEM_SPEC,
        SMEM_SPEC,
        tiles(block, (h, wd, c)),
        whole(edges.shape),
        whole(w.shape),
    ]
    shapes = [
        jax.ShapeDtypeStruct((n, h + 2, wd, 3 * c), bf16),
        jax.ShapeDtypeStruct((n, h * wd, c), f32),
        jax.ShapeDtypeStruct((n, h * wd, c) if last else (n, h, wd, c), bf16),
    ]
    args = [index, flips, x, edges, w]
    scratch = [VMEM((h + 2, wd + 16, c), f32)]
    if last:
        in_specs.append(whole(head_t.shape))
        args.append(head_t)
        shapes.append(jax.ShapeDtypeStruct((n, head_t.shape[0], h * wd), bf16))
    else:
        shapes.append(jax.ShapeDtypeStruct((n, 4, wd, c), bf16))
        scratch.append(VMEM((h, wd, c), f32))
    return pl.pallas_call(
        functools.partial(conv_kernel, block, last),
        grid=(n // block,),
        out_shape=shapes,
        in_specs=in_specs,
        out_specs=[tiles(block, s.shape[1:]) for s in shapes],
        scratch_shapes=scratch,
        compiler_params=pltpu.CompilerParams(vmem_limit_bytes=LIMIT),
        name="conv_last" if last else "conv_first",
    )(*args)


def back_kernel(block, ensemble, tile_dev, h, w, *refs):
    y_ref, own_ref, obs_ref, act_ref, pre_ref, head_ref, w_ref = refs[:7]
    slope_ref, inner_ref, side_ref, hg_ref, va, vb, pad, s3, cols = refs[7:]
    c = act_ref.shape[-1]
    step = pl.program_id(0)

    @pl.when(step == 0)
    def _():
        hg_ref[...] = jnp.zeros_like(hg_ref)
        for a in range(3):
            for b in range(3):
                tap = w_ref[(3 * a + b) * c : (3 * a + b + 1) * c, :]
                va[a, :, b * c : (b + 1) * c] = tap
                if b == 0:
                    vb[0, :, a * c : (a + 1) * c] = tap
                if b == 2:
                    vb[1, :, a * c : (a + 1) * c] = tap
        pad[...] = jnp.zeros_like(pad)

    for k in range(block):
        t = (step * block + k) % tile_dev
        y = own_ref[k].astype(f32)

        def g(x):
            return x * lax.rsqrt(x * x + smooth_sq)

        gap = g(y - obs_ref[t].astype(f32))
        paired = jnp.zeros_like(y)
        for m in range(ensemble):
            paired = paired + g(y - y_ref[m, t].astype(f32))
        slope_out = ((gap / ensemble - paired / (ensemble * ensemble)) / h).astype(bf16)
        hg_ref[...] += mm(slope_out, act_ref[k])
        back = mm(slope_out, head_ref[...], TN)
        slope = (back * dsilu(pre_ref[k])).astype(bf16)
        slope_ref[k] = slope
        pad[2 : h + 2, 8 : 8 + w, :] = slope.astype(f32).reshape(h, w, c)
        for b in range(3):
            s3[k, :, :, b * c : (b + 1) * c] = pad[:, 9 - b : 9 - b + w, :].astype(bf16)
        left = pad[:, 8:9, :].reshape(h + 4, c)
        right = pad[:, 7 + w : 8 + w, :].reshape(h + 4, c)
        for a in range(3):
            cols[0, k, :, a * c : (a + 1) * c] = left[3 - a : 3 - a + h].astype(bf16)
            cols[1, k, :, a * c : (a + 1) * c] = right[3 - a : 3 - a + h].astype(bf16)
    full = None
    for a in range(3):
        part = mm(s3[:, 2 - a : 20 - a + h - 16].reshape(block * (h + 2) * w, 3 * c), va[a], NT)
        full = part if full is None else full + part
    full = full.reshape(block, h + 2, w, c).astype(bf16)
    inner_ref[...] = full[:, 1 : h + 1]
    lefts = mm(cols[0].reshape(block * h, 3 * c), vb[0], NT).astype(bf16)
    rights = mm(cols[1].reshape(block * h, 3 * c), vb[1], NT).astype(bf16)
    for k in range(block):
        side_ref[k, 0] = full[k, 0]
        side_ref[k, 1] = rights[k * h : (k + 1) * h]
        side_ref[k, 2] = full[k, h + 1]
        side_ref[k, 3] = lefts[k * h : (k + 1) * h]


def backward(y_all, own, obs, act, pre, head_t, w, h, wd):
    n, cells, c = act.shape
    ensemble, tile_dev = y_all.shape[:2]
    block = block_of(n)
    shapes = [
        jax.ShapeDtypeStruct((n, cells, c), bf16),
        jax.ShapeDtypeStruct((n, h, wd, c), bf16),
        jax.ShapeDtypeStruct((n, 4, wd, c), bf16),
        jax.ShapeDtypeStruct(head_t.shape, f32),
    ]
    return pl.pallas_call(
        functools.partial(back_kernel, block, ensemble, tile_dev, h, wd),
        grid=(n // block,),
        out_shape=shapes,
        in_specs=[
            whole(y_all.shape),
            tiles(block, own.shape[1:]),
            whole(obs.shape),
            tiles(block, (cells, c)),
            tiles(block, (cells, c)),
            whole(head_t.shape),
            whole(w.shape),
        ],
        out_specs=[tiles(block, s.shape[1:]) for s in shapes[:3]] + [whole(head_t.shape)],
        scratch_shapes=[
            VMEM((3, c, 3 * c), bf16),
            VMEM((2, c, 3 * c), bf16),
            VMEM((h + 4, wd + 16, c), f32),
            VMEM((block, h + 4, wd, 3 * c), bf16),
            VMEM((2, block, h, 3 * c), bf16),
        ],
        compiler_params=pltpu.CompilerParams(vmem_limit_bytes=LIMIT),
        name="backward",
    )(y_all, own, obs, act, pre, head_t, w)


def grad_kernel(block, steps, mid, h, w, *refs):
    if mid:
        index_ref, flip_ref, edges_ref, inner_ref, pre_ref, x3_ref, out_ref, acc, field = refs
    else:
        slope_ref, x3_ref, out_ref, acc = refs
    c = out_ref.shape[-1]
    step = pl.program_id(0)

    @pl.when(step == 0)
    def _():
        acc[...] = jnp.zeros_like(acc)

    slopes = []
    for k in range(block):
        if mid:
            rims = rims_of(index_ref, flip_ref, edges_ref, step * block + k, w)
            field[...] = inner_ref[k].astype(f32)
            field[0] += rims[0:w]
            field[:, w - 1 : w, :] += rims[w : w + h].reshape(h, 1, c)
            field[h - 1] += rims[w + h : 2 * w + h]
            field[:, 0:1, :] += rims[2 * w + h :].reshape(h, 1, c)
            slope = (field[...].reshape(h * w, c) * dsilu(pre_ref[k])).astype(bf16)
        else:
            slope = slope_ref[k]
        slopes.append(slope.T)
    turned = jnp.concatenate(slopes, axis=1)
    for a in range(3):
        acc[a] += mm(turned, x3_ref[:, a : a + h].reshape(block * h * w, 3 * c))

    @pl.when(step == steps - 1)
    def _():
        for a in range(3):
            for b in range(3):
                out_ref[(3 * a + b) * c : (3 * a + b + 1) * c, :] = acc[
                    a, :, b * c : (b + 1) * c
                ].T


def weight_grad(x3, h, w, c, slope=None, mid=None):
    n = x3.shape[0]
    block = block_of(n)
    steps = n // block
    scratch = [VMEM((3, c, 3 * c), f32)]
    if mid is None:
        args = [slope, x3]
        in_specs = [tiles(block, slope.shape[1:]), tiles(block, x3.shape[1:])]
    else:
        index, flips, edges, inner, pre = mid
        args = [index, flips, edges, inner, pre, x3]
        in_specs = [
            SMEM_SPEC,
            SMEM_SPEC,
            whole(edges.shape),
            tiles(block, inner.shape[1:]),
            tiles(block, pre.shape[1:]),
            tiles(block, x3.shape[1:]),
        ]
        scratch.append(VMEM((h, w, c), f32))
    return pl.pallas_call(
        functools.partial(grad_kernel, block, steps, mid is not None, h, w),
        grid=(steps,),
        out_shape=jax.ShapeDtypeStruct((9 * c, c), f32),
        in_specs=in_specs,
        out_specs=whole((9 * c, c)),
        scratch_shapes=scratch,
        compiler_params=pltpu.CompilerParams(vmem_limit_bytes=LIMIT),
        name="grad_two" if mid is None else "grad_one",
    )(*args)


def split_edges(x):
    return jnp.stack([x[:, 0], x[:, :, -1], x[:, -1], x[:, :, 0]], axis=1)


def edge_table(adjacency, placement_map, first_slot, members, tile_dev):
    total = placement_map.shape[0]
    ids = jnp.arange(total, dtype=jnp.int32)
    mine = first_slot + jnp.arange(tile_dev, dtype=jnp.int32)
    my_tiles = jnp.sum(jnp.where(ids[None] == mine[:, None], placement_map[None], 0), axis=1)
    hit = ids[None, :] == my_tiles[:, None]
    entries = jnp.sum(jnp.where(hit[:, :, None, None], adjacency[None], 0), axis=1)
    neighbour, side, flip = entries[:, :, 0], entries[:, :, 1], entries[:, :, 2]
    found = neighbour[:, :, None] == placement_map[None, None, :]
    slot = jnp.sum(jnp.where(found, ids[None, None, :], 0), axis=2)
    face, inner = slot // tile_dev, slot % tile_dev
    m = jnp.arange(members, dtype=jnp.int32)[:, None, None]
    index = ((face[None] * members + m) * tile_dev + inner[None]) * 4 + side[None]
    flips = jnp.broadcast_to(flip[None], index.shape)
    return index.reshape(-1), flips.reshape(-1)


def shards(faces, zs, features, observed, conv_weights, head_weight, adjacency, placement_map):
    members, tile_dev, h, w, c = features.shape
    n = members * tile_dev
    variables = head_weight.shape[1]
    index, flips = edge_table(
        adjacency, placement_map, lax.axis_index("face") * tile_dev, members, tile_dev
    )
    x = features.reshape(n, h, w, c)
    rows = conv_weights.shape[0]
    head_rows = head_weight.shape[0]
    lanes = -(-variables // 128) * 128
    head_wide = jnp.pad(head_weight, ((0, 0), (0, lanes - variables)))
    edges, w0, w1, head = first_gather(
        split_edges(x), [conv_weights[:, 0], conv_weights[:, 1], head_wide], faces, zs
    )
    w0 = w0.reshape(faces * zs * rows, c)
    w1 = w1.reshape(faces * zs * rows, c)
    head_t = head.reshape(faces * zs * head_rows, lanes)[:, :variables].T
    obs = lax.all_gather(observed, "member", axis=2, tiled=True)

    def flat(e):
        return e.reshape((faces * n * 4,) + e.shape[-2:])

    x3_one, pre_one, act_one, sides = conv(index, flips, x, flat(edges), w0)
    x3_two, pre_two, act_two, outs = conv(
        index, flips, act_one, flat(face_gather(sides, faces, 2)), w1, head_t
    )
    y_all = member_gather(outs, zs, 3).reshape(zs * members, tile_dev, variables, h * w)
    slope_two, inner, borders, hg = backward(
        y_all, outs, obs, act_two, pre_two, head_t, w1, h, w
    )
    grad_two = weight_grad(x3_two, h, w, c, slope=slope_two)
    returned = flat(face_gather(borders, faces, 4))
    grad_one = weight_grad(x3_one, h, w, c, mid=(index, flips, returned, inner, pre_one))
    hg = jnp.pad(hg.T, ((0, 0), (0, lanes - variables)))
    chips = faces // 2
    one, two, head_out = scatter(
        [
            grad_one.reshape(chips, 2, zs, rows, c),
            grad_two.reshape(chips, 2, zs, rows, c),
            hg.reshape(chips, 2, zs, head_rows, lanes),
        ],
        faces,
        zs,
        5,
    )
    return jnp.stack([one, two], axis=1), head_out[:, :variables]


def solution(mesh):
    in_specs = (
        P("member", "face", None, None, None),
        P("face", None, "member"),
        P(("face", "member"), None, None),
        P(("face", "member"), None),
        P(),
        P(),
    )
    out_specs = (P(("face", "member"), None, None), P(("face", "member"), None))
    body = functools.partial(shards, mesh.shape["face"], mesh.shape["member"])
    return jax.shard_map(body, mesh=mesh, in_specs=in_specs, out_specs=out_specs, check_vma=False)
```

```python
import functools

import jax
import jax.numpy as jnp
from jax import lax
from jax.experimental import pallas as pl
from jax.experimental.pallas import tpu as pltpu
from jax.sharding import PartitionSpec as P

smooth_sq = 0.0625
MESH = pl.DeviceIdType.MESH
VMEM = pltpu.VMEM
f32 = jnp.float32
bf16 = jnp.bfloat16
LIMIT = 60 * 1024 * 1024
NT = (((1,), (1,)), ((), ()))
TN = (((0,), (0,)), ((), ()))
NN = (((1,), (0,)), ((), ()))


def mm(a, b, dims=NN):
    return lax.dot_general(a, b, dims, preferred_element_type=f32)


def rcopy(src, dst, send, recv, **where):
    return pltpu.make_async_remote_copy(
        src_ref=src, dst_ref=dst, send_sem=send, recv_sem=recv, device_id=where, device_id_type=MESH
    )


def greet(chips, members, face_axis, member_axis):
    face = lax.axis_index("face")
    member = lax.axis_index("member")
    core = face % 2
    chip = face // 2
    barrier = pltpu.get_barrier_semaphore()
    count = 0
    if face_axis:
        pl.semaphore_signal(
            barrier, inc=1, device_id={"face": chip * 2 + 1 - core}, device_id_type=MESH
        )
        for j in range(1, chips):
            pl.semaphore_signal(
                barrier,
                inc=1,
                device_id={"face": ((chip + j) % chips) * 2 + core},
                device_id_type=MESH,
            )
        count += chips
    if member_axis:
        for j in range(1, members):
            pl.semaphore_signal(
                barrier, inc=1, device_id={"member": (member + j) % members}, device_id_type=MESH
            )
        count += members - 1
    pl.semaphore_wait(barrier, count)


def line_gather(x_ref, out_at, member, members, sems):
    ups, upr, dns, dnr = sems
    steps = members - 1

    def up(s):
        b = jnp.maximum(member - s, 0)
        return rcopy(
            x_ref if s == 0 else out_at(b),
            out_at(b),
            ups.at[s],
            upr.at[s],
            member=jnp.minimum(member + 1, members - 1),
        )

    def down(s):
        b = jnp.minimum(member + s, members - 1)
        return rcopy(
            x_ref if s == 0 else out_at(b),
            out_at(b),
            dns.at[s],
            dnr.at[s],
            member=jnp.maximum(member - 1, 0),
        )

    def up_goes(s):
        return jnp.logical_and(member - s >= 0, member < members - 1)

    def down_goes(s):
        return jnp.logical_and(member + s < members, member > 0)

    pl.when(up_goes(0))(lambda: up(0).start())
    pl.when(down_goes(0))(lambda: down(0).start())
    for s in range(steps):
        pl.when(member - 1 - s >= 0)(lambda: up(s).wait_recv())
        if s + 1 < steps:
            pl.when(up_goes(s + 1))(lambda: up(s + 1).start())
        pl.when(member + 1 + s < members)(lambda: down(s).wait_recv())
        if s + 1 < steps:
            pl.when(down_goes(s + 1))(lambda: down(s + 1).start())
    for s in range(steps):
        pl.when(up_goes(s))(lambda: up(s).wait_send())
        pl.when(down_goes(s))(lambda: down(s).wait_send())


class FaceGather:
    def __init__(self, src, out, chips, sems):
        self.src, self.out, self.chips = src, out, chips
        self.send, self.recv, self.fsend, self.frecv = sems
        face = lax.axis_index("face")
        self.face, self.core, self.chip = face, face % 2, face // 2
        self.partner = self.chip * 2 + 1 - self.core

    def direct(self, j):
        return rcopy(
            self.src,
            self.out.at[self.face],
            self.send.at[j],
            self.recv.at[j],
            face=((self.chip + j) % self.chips) * 2 + self.core,
        )

    def forward(self, j):
        block = ((self.chip + self.chips - j) % self.chips) * 2 + self.core
        return rcopy(
            self.src if j == 0 else self.out.at[block],
            self.out.at[block],
            self.fsend.at[j],
            self.frecv.at[j],
            face=self.partner,
        )

    def start(self):
        for j in range(1, self.chips):
            self.direct(j).start()
        self.forward(0).start()

    def relay(self):
        self.relay_first()
        self.relay_rest()

    def relay_first(self):
        pass

    def relay_rest(self):
        for j in range(1, self.chips):
            self.direct(j).wait_recv()
            self.forward(j).start()

    def finish(self):
        for j in range(1, self.chips):
            self.direct(j).wait_send()
        for j in range(self.chips):
            self.forward(j).wait()


class SquareGather:
    def __init__(self, src, out, chips, sems):
        self.src, self.out = src, out
        self.send, self.recv, self.fsend, self.frecv = sems
        face = lax.axis_index("face")
        core, chip = face % 2, face // 2
        col, row = chip % 2, chip // 2
        self.face = face
        self.partner = chip * 2 + 1 - core
        self.beside = (row * 2 + 1 - col) * 2 + core
        self.below = ((1 - row) * 2 + col) * 2 + core
        self.across = ((1 - row) * 2 + 1 - col) * 2 + core
        self.half = src.shape[0] // 2

    def part(self, k):
        return pl.ds((0, 1, 1, 0, 0, 1)[k] * self.half, self.half)

    def came(self, k):
        block = (self.beside, self.beside, self.below, self.below, self.across, self.across)[k]
        return self.out.at[block, self.part(k)]

    def direct(self, k):
        to = (self.beside, self.beside, self.below, self.below, self.below, self.beside)[k]
        if k < 4:
            src, block = self.src.at[self.part(k)], self.face
        else:
            block = self.beside if k == 4 else self.below
            src = self.out.at[block, self.part(k)]
        return rcopy(
            src, self.out.at[block, self.part(k)], self.send.at[k], self.recv.at[k], face=to
        )

    def forward(self, k):
        if k == 6:
            src, dst = self.src, self.out.at[self.face]
        else:
            src = dst = self.came(k)
        return rcopy(src, dst, self.fsend.at[k], self.frecv.at[k], face=self.partner)

    def start(self):
        for k in (0, 2, 1, 3):
            self.direct(k).start()
        self.forward(6).start()

    def relay(self):
        self.relay_first()
        self.relay_rest()

    def relay_first(self):
        for k, onward in ((0, 4), (2, 5)):
            self.direct(k).wait_recv()
            self.direct(onward).start()
            self.forward(k).start()

    def relay_rest(self):
        for k in (1, 3, 4, 5):
            self.direct(k).wait_recv()
            self.forward(k).start()

    def finish(self):
        for k in range(6):
            self.direct(k).wait_send()
        for k in range(7):
            self.forward(k).wait()


def gather_over_face(src, out, chips, sems):
    kind = SquareGather if chips == 4 and src.shape[0] % 2 == 0 else FaceGather
    return kind(src, out, chips, sems)


def dma_sems(*sizes):
    return [pltpu.SemaphoreType.DMA((max(n, 1),)) for n in sizes]


def first_gather_kernel(chips, members, count, *refs):
    x, ws = refs[0], refs[1 : 1 + count]
    edges_out, outs = refs[1 + count], refs[2 + count : 2 + 2 * count]
    edges, field, own_sem = refs[2 + 2 * count : 5 + 2 * count]
    sems = refs[5 + 2 * count :]
    face = lax.axis_index("face")
    member = lax.axis_index("member")
    own = []
    for k in range(count):
        own.append(
            pltpu.make_async_copy(ws[k], outs[k].at[face, member], own_sem.at[k + 1])
        )
        own[k].start()

    def cut(k, carry):
        field[...] = x[k].astype(f32)
        sides_out(field, edges, k)
        return carry

    lax.fori_loop(0, x.shape[0], cut, 0)
    greet(chips, members, True, True)
    eg = gather_over_face(edges, edges_out, chips, sems[:4])
    eg.start()
    edges_out[face] = edges[...]
    for c in own:
        c.wait()
    rest = sems[4:]
    wgs = []
    for k in range(count):
        line = rest[8 * k : 8 * k + 4]
        line_gather(ws[k], lambda b: outs[k].at[face, b], member, members, line)
        wg = gather_over_face(outs[k].at[face], outs[k], chips, rest[8 * k + 4 : 8 * k + 8])
        wg.start()
        wgs.append(wg)
        if k == 0:
            eg.relay_first()
    eg.relay_rest()
    for wg in wgs:
        wg.relay()
    eg.finish()
    for wg in wgs:
        wg.finish()


def first_gather(x, ws, faces, members):
    chips = faces // 2
    count = len(ws)
    n, h, w, c = x.shape
    shapes = [jax.ShapeDtypeStruct((faces, n, 4, w, c), x.dtype)] + [
        jax.ShapeDtypeStruct((faces, members) + v.shape, v.dtype) for v in ws
    ]
    scratch = [VMEM((n, 4, w, c), x.dtype), VMEM((h, w, c), f32)]
    scratch += dma_sems(count + 1) + dma_sems(*([chips + 3] * 4))
    for _ in ws:
        scratch += dma_sems(*([members] * 4)) + dma_sems(*([chips + 3] * 4))
    return pl.pallas_call(
        functools.partial(first_gather_kernel, chips, members, count),
        out_shape=shapes,
        in_specs=[pl.BlockSpec(memory_space=VMEM)] * (count + 1),
        out_specs=[pl.BlockSpec(memory_space=VMEM)] * (count + 1),
        scratch_shapes=scratch,
        compiler_params=pltpu.CompilerParams(
            collective_id=1, has_side_effects=True, vmem_limit_bytes=LIMIT
        ),
        name="first_gather",
    )(x, *ws)


def face_gather_kernel(chips, x, out, own_sem, *sems):
    own = pltpu.make_async_copy(x, out.at[lax.axis_index("face")], own_sem.at[0])
    own.start()
    greet(chips, 1, True, False)
    g = gather_over_face(x, out, chips, sems)
    g.start()
    own.wait()
    g.relay()
    g.finish()


def face_gather(x, faces, ident):
    chips = faces // 2
    return pl.pallas_call(
        functools.partial(face_gather_kernel, chips),
        out_shape=jax.ShapeDtypeStruct((faces,) + x.shape, x.dtype),
        in_specs=[pl.BlockSpec(memory_space=VMEM)],
        out_specs=pl.BlockSpec(memory_space=VMEM),
        scratch_shapes=dma_sems(1) + dma_sems(*([chips + 3] * 4)),
        compiler_params=pltpu.CompilerParams(
            collective_id=ident, has_side_effects=True, vmem_limit_bytes=LIMIT
        ),
        name="face_gather",
    )(x)


def score_kernel(members, held, tile_dev, chunk, h, *refs):
    y, obs, out, packed, came, slopes, back = refs[:7]
    s1, r1, s2, r2 = refs[7:]
    member = lax.axis_index("member")
    part = obs.shape[-1]
    ensemble = held * members
    chunks = tile_dev // chunk

    def there(j):
        return (member + j) % members

    def source(j):
        return (member + members - j) % members

    def go(i, j):
        at = pl.ds(i * chunk, chunk)
        return rcopy(
            packed.at[there(j), at], came.at[j, at], s1.at[i, j], r1.at[i, j], member=there(j)
        )

    def home(i, j):
        at = pl.ds(i * chunk, chunk)
        return rcopy(
            slopes.at[j, at], back.at[member, at], s2.at[i, j], r2.at[i, j], member=source(j)
        )

    def home_here(i, j):
        at = pl.ds(i * chunk, chunk)
        return rcopy(
            slopes.at[j, at], back.at[there(j), at], s2.at[i, j], r2.at[i, j], member=source(j)
        )

    def pack(t):
        for q in range(members):
            packed[q, t] = jnp.concatenate(
                [y[m * tile_dev + t][:, q * part : (q + 1) * part] for m in range(held)], axis=1
            )

    def g(v):
        return v * lax.rsqrt(v * v + smooth_sq)

    def score(t):
        o = obs[t].astype(f32)
        o = jnp.concatenate([o] * held, axis=1)
        vals = [packed[member, t].astype(f32)]
        vals += [came[j, t].astype(f32) for j in range(1, members)]
        turned = [
            jnp.concatenate([v[:, k * part :], v[:, : k * part]], axis=1) if k else v
            for v in vals
            for k in range(held)
        ]
        for j in range(members):
            v = vals[j]
            paired = jnp.zeros_like(v)
            for u in turned:
                paired = paired + g(v - u)
            s = (g(v - o) / ensemble - paired / (ensemble * ensemble)) / h
            s = s.astype(bf16)
            if j == 0:
                back[member, t] = s
            else:
                slopes[j, t] = s

    pack_first = [pack(t) for t in range(chunk)]
    del pack_first
    greet(1, members, False, True)
    for i in range(chunks):
        if i:
            for t in range(i * chunk, (i + 1) * chunk):
                pack(t)
        for j in range(1, members):
            go(i, j).start()
    for i in range(chunks):
        for j in range(1, members):
            go(i, j).wait_recv()
        for t in range(i * chunk, (i + 1) * chunk):
            score(t)
        for j in range(1, members):
            home(i, j).start()
    for i in range(chunks):
        for j in range(1, members):
            home_here(i, j).wait_recv()
        for t in range(i * chunk, (i + 1) * chunk):
            for m in range(held):
                out[m * tile_dev + t] = jnp.concatenate(
                    [back[q, t][:, m * part : (m + 1) * part] for q in range(members)], axis=1
                )
    for i in range(chunks):
        for j in range(1, members):
            go(i, j).wait_send()
            home(i, j).wait_send()


def score_exchange(y, obs, members, h, ident):
    n, variables, cells = y.shape
    tile_dev = obs.shape[0]
    held = n // tile_dev
    chunk = 2 if tile_dev % 2 == 0 else 1
    wide = (members, tile_dev, variables, held * obs.shape[-1])
    sems = pltpu.SemaphoreType.DMA((tile_dev // chunk, members))
    return pl.pallas_call(
        functools.partial(score_kernel, members, held, tile_dev, chunk, h),
        out_shape=jax.ShapeDtypeStruct(y.shape, bf16),
        in_specs=[pl.BlockSpec(memory_space=VMEM)] * 2,
        out_specs=pl.BlockSpec(memory_space=VMEM),
        scratch_shapes=[VMEM(wide, bf16)] * 4 + [sems] * 4,
        compiler_params=pltpu.CompilerParams(
            collective_id=ident, has_side_effects=True, vmem_limit_bytes=LIMIT
        ),
        name="score",
    )(y, obs)


def scatter_kernel(chips, members, count, *refs):
    gs, outs = refs[:count], refs[count : 2 * count]
    scratch = refs[2 * count :]
    face = lax.axis_index("face")
    member = lax.axis_index("member")
    core, chip = face % 2, face // 2
    partner = chip * 2 + 1 - core
    greet(chips, members, True, True)

    def parts(k):
        return scratch[10 * k : 10 * k + 10]

    def there(j):
        return (chip + j) % chips

    def core_copy(k, j):
        fromcore, _, _, _, s0, r0, _, _, _, _ = parts(k)
        return rcopy(
            gs[k].at[there(j), 1 - core], fromcore.at[j], s0.at[j], r0.at[j], face=partner
        )

    def chip_copy(k, j):
        _, acc, fromchip, _, _, _, s1, r1, _, _ = parts(k)
        return rcopy(acc.at[j], fromchip.at[j], s1.at[j], r1.at[j], face=there(j) * 2 + core)

    def line_copy(k, j):
        _, acc, _, fromline, _, _, _, _, s2, r2 = parts(k)
        to = (member + j) % members
        return rcopy(acc.at[0, to], fromline.at[j], s2.at[j], r2.at[j], member=to)

    order = list(range(1, chips)) + [0]
    for k in range(count):
        for j in order:
            core_copy(k, j).start()
    for k in range(count):
        fromcore, acc = parts(k)[:2]
        for j in order:
            core_copy(k, j).wait_recv()
            acc[j] = gs[k][there(j), core] + fromcore[j]
            if j:
                chip_copy(k, j).start()
    for k in range(count):
        acc, fromchip = parts(k)[1:3]
        for j in range(1, chips):
            chip_copy(k, j).wait_recv()
            acc[0] = acc[0] + fromchip[j]
        for j in range(1, members):
            line_copy(k, j).start()
    for k in range(count):
        acc, fromline = parts(k)[1], parts(k)[3]
        total = acc[0, member]
        for j in range(1, members):
            line_copy(k, j).wait_recv()
            total = total + fromline[j]
        outs[k][...] = total
    for k in range(count):
        for j in range(chips):
            core_copy(k, j).wait_send()
        for j in range(1, chips):
            chip_copy(k, j).wait_send()
        for j in range(1, members):
            line_copy(k, j).wait_send()


def scatter(gs, faces, members, ident):
    chips = faces // 2
    scratch = []
    for g in gs:
        tail = g.shape[3:]
        scratch += [
            VMEM((chips, members) + tail, f32),
            VMEM((chips, members) + tail, f32),
            VMEM((chips, members) + tail, f32),
            VMEM((members,) + tail, f32),
        ] + dma_sems(chips, chips, chips, chips, members, members)
    return pl.pallas_call(
        functools.partial(scatter_kernel, chips, members, len(gs)),
        out_shape=[jax.ShapeDtypeStruct(g.shape[3:], f32) for g in gs],
        in_specs=[pl.BlockSpec(memory_space=VMEM)] * len(gs),
        out_specs=[pl.BlockSpec(memory_space=VMEM)] * len(gs),
        scratch_shapes=scratch,
        compiler_params=pltpu.CompilerParams(
            collective_id=ident, has_side_effects=True, vmem_limit_bytes=LIMIT
        ),
        name="scatter",
    )(*gs)


def rims_of(index_ref, flip_ref, edges_ref, n, length):
    cat = jnp.concatenate([edges_ref[index_ref[n * 4 + a]] for a in range(4)], axis=0)
    size = 4 * length
    row = lax.broadcasted_iota(jnp.int32, (size, size), 0)
    col = lax.broadcasted_iota(jnp.int32, (size, size), 1)
    side = row // length
    place = row - side * length
    flag = jnp.zeros((size, size), jnp.int32)
    for a in range(4):
        flag = jnp.where(side == a, flip_ref[n * 4 + a], flag)
    target = side * length + jnp.where(flag == 1, length - 1 - place, place)
    return mm(jnp.where(col == target, 1.0, 0.0).astype(bf16), cat)


def col_to_rows(ref_slice):
    height, _, channels = ref_slice.shape
    return ref_slice.reshape(height, channels)


def sides_out(field, edge_ref, k):
    w = field.shape[1]
    h = field.shape[0]
    edge_ref[k, 0] = field[0].astype(bf16)
    edge_ref[k, 1] = col_to_rows(field[:, w - 1 : w, :]).astype(bf16)
    edge_ref[k, 2] = field[h - 1].astype(bf16)
    edge_ref[k, 3] = col_to_rows(field[:, 0:1, :]).astype(bf16)


def silu(v):
    return v / (1.0 + jnp.exp(-v))


def dsilu(v):
    s = 1.0 / (1.0 + jnp.exp(-v))
    return s * (1.0 + v * (1.0 - s))


def table(place_ref, glue_ref, index_ref, flip_ref, slot_of, members, tile_dev):
    first = lax.axis_index("face") * tile_dev

    def invert(s, carry):
        slot_of[place_ref[s]] = s
        return carry

    lax.fori_loop(0, place_ref.shape[0], invert, 0)

    def fill(i, carry):
        tile = place_ref[first + i]
        for a in range(4):
            base = (tile * 4 + a) * 3
            slot = slot_of[glue_ref[base]]
            face = slot // tile_dev
            inner = slot - face * tile_dev
            for m in range(members):
                at = (m * tile_dev + i) * 4 + a
                index_ref[at] = ((face * members + m) * tile_dev + inner) * 4 + glue_ref[base + 1]
                flip_ref[at] = glue_ref[base + 2]
        return carry

    lax.fori_loop(0, tile_dev, fill, 0)


def conv_kernel(block, members, *refs):
    last = members is None
    if last:
        index_ref, flip_ref, x_ref, edges_ref, w_ref = refs[:5]
        head_ref, x3_ref, pre_ref, act_ref, out_ref, pad = refs[5:]
    else:
        place_ref, glue_ref, x_ref, edges_ref, w_ref = refs[:5]
        x3_ref, pre_ref, act_ref, side_ref, index_ref, flip_ref, pad, field, slot_of = refs[5:]
    _, h, w, c = x_ref.shape
    step = pl.program_id(0)
    if not last:
        tile_dev = index_ref.shape[0] // (4 * members)
        pl.when(step == 0)(
            lambda: table(place_ref, glue_ref, index_ref, flip_ref, slot_of, members, tile_dev)
        )
    for k in range(block):
        n = step * block + k
        rims = rims_of(index_ref, flip_ref, edges_ref, n, w)
        zero = jnp.zeros((8, c), f32)
        for r in (0, h + 1):
            pad[r, 0:8, :] = zero
            pad[r, 8 + w : 16 + w, :] = zero
        pad[1 : h + 1, 8 : 8 + w, :] = x_ref[k].astype(f32)
        pad[0, 8 : 8 + w, :] = rims[0:w]
        pad[1 : h + 1, 8 + w : 9 + w, :] = rims[w : w + h].reshape(h, 1, c)
        pad[h + 1, 8 : 8 + w, :] = rims[w + h : 2 * w + h]
        pad[1 : h + 1, 7:8, :] = rims[2 * w + h :].reshape(h, 1, c)
        for b in range(3):
            x3_ref[k, :, :, b * c : (b + 1) * c] = pad[:, 7 + b : 7 + b + w, :].astype(bf16)
    pre = None
    for a in range(3):
        part = mm(
            x3_ref[:, a : a + h].reshape(block * h * w, 3 * c),
            w_ref[3 * a * c : 3 * (a + 1) * c, :],
        )
        pre = part if pre is None else pre + part
    pre_ref[...] = pre.reshape(block, h * w, c)
    act = silu(pre).astype(bf16)
    act_ref[...] = act.reshape(act_ref.shape)
    if last:
        for k in range(block):
            out_ref[k] = mm(head_ref[...], act[k * h * w : (k + 1) * h * w], NT).astype(bf16)
    else:
        for k in range(block):
            field[...] = act[k * h * w : (k + 1) * h * w].astype(f32).reshape(h, w, c)
            sides_out(field, side_ref, k)


def whole(shape):
    return pl.BlockSpec(shape, lambda i: (0,) * len(shape))


def tiles(block, shape):
    return pl.BlockSpec((block,) + shape, lambda i: (i,) + (0,) * len(shape))


SMEM_SPEC = pl.BlockSpec(memory_space=pltpu.SMEM)


def block_of(n):
    return 3 if n % 3 == 0 else (2 if n % 2 == 0 else 1)


def layer(shape, which):
    return pl.BlockSpec((shape[0], shape[1] // 2), lambda i: (0, which))


def conv(scalars, x, edges, w, members=None, head_t=None):
    n, h, wd, c = x.shape
    block = block_of(n)
    last = members is None
    in_specs = [
        SMEM_SPEC,
        SMEM_SPEC,
        tiles(block, (h, wd, c)),
        whole(edges.shape),
        layer(w.shape, int(last)),
    ]
    shapes = [
        jax.ShapeDtypeStruct((n, h + 2, wd, 3 * c), bf16),
        jax.ShapeDtypeStruct((n, h * wd, c), f32),
        jax.ShapeDtypeStruct((n, h * wd, c) if last else (n, h, wd, c), bf16),
    ]
    args = [*scalars, x, edges, w]
    scratch = [VMEM((h + 2, wd + 16, c), f32)]
    if last:
        in_specs.append(whole(head_t.shape))
        args.append(head_t)
        shapes.append(jax.ShapeDtypeStruct((n, head_t.shape[0], h * wd), bf16))
    else:
        shapes.append(jax.ShapeDtypeStruct((n, 4, wd, c), bf16))
        scratch.append(VMEM((h, wd, c), f32))
        scratch.append(pltpu.SMEM(scalars[0].shape, jnp.int32))
    out_specs = [tiles(block, s.shape[1:]) for s in shapes]
    if not last:
        shapes += [jax.ShapeDtypeStruct((n * 4,), jnp.int32)] * 2
        out_specs += [SMEM_SPEC] * 2
    return pl.pallas_call(
        functools.partial(conv_kernel, block, members),
        grid=(n // block,),
        out_shape=shapes,
        in_specs=in_specs,
        out_specs=out_specs,
        scratch_shapes=scratch,
        compiler_params=pltpu.CompilerParams(vmem_limit_bytes=LIMIT),
        name="conv_last" if last else "conv_first",
    )(*args)


def back_kernel(block, h, w, *refs):
    out_ref, act_ref, pre_ref, head_ref, w_ref = refs[:5]
    slope_ref, inner_ref, side_ref, hg_ref, va, vb, pad, s3, cols = refs[5:]
    c = act_ref.shape[-1]
    step = pl.program_id(0)

    @pl.when(step == 0)
    def _():
        hg_ref[...] = jnp.zeros_like(hg_ref)
        for a in range(3):
            for b in range(3):
                tap = w_ref[(3 * a + b) * c : (3 * a + b + 1) * c, :]
                va[a, :, b * c : (b + 1) * c] = tap
                if b == 0:
                    vb[0, :, a * c : (a + 1) * c] = tap
                if b == 2:
                    vb[1, :, a * c : (a + 1) * c] = tap
        pad[...] = jnp.zeros_like(pad)

    for k in range(block):
        slope_out = out_ref[k]
        hg_ref[...] += mm(slope_out, act_ref[k])
        back = mm(slope_out, head_ref[...], TN)
        slope = (back * dsilu(pre_ref[k])).astype(bf16)
        slope_ref[k] = slope
        pad[2 : h + 2, 8 : 8 + w, :] = slope.astype(f32).reshape(h, w, c)
        for b in range(3):
            s3[k, :, :, b * c : (b + 1) * c] = pad[:, 9 - b : 9 - b + w, :].astype(bf16)
        left = pad[:, 8:9, :].reshape(h + 4, c)
        right = pad[:, 7 + w : 8 + w, :].reshape(h + 4, c)
        for a in range(3):
            cols[0, k, :, a * c : (a + 1) * c] = left[3 - a : 3 - a + h].astype(bf16)
            cols[1, k, :, a * c : (a + 1) * c] = right[3 - a : 3 - a + h].astype(bf16)
    full = None
    for a in range(3):
        part = mm(s3[:, 2 - a : 20 - a + h - 16].reshape(block * (h + 2) * w, 3 * c), va[a], NT)
        full = part if full is None else full + part
    full = full.reshape(block, h + 2, w, c).astype(bf16)
    inner_ref[...] = full[:, 1 : h + 1]
    lefts = mm(cols[0].reshape(block * h, 3 * c), vb[0], NT).astype(bf16)
    rights = mm(cols[1].reshape(block * h, 3 * c), vb[1], NT).astype(bf16)
    for k in range(block):
        side_ref[k, 0] = full[k, 0]
        side_ref[k, 1] = rights[k * h : (k + 1) * h]
        side_ref[k, 2] = full[k, h + 1]
        side_ref[k, 3] = lefts[k * h : (k + 1) * h]


def backward(slope_out, act, pre, head_t, w, h, wd):
    n, cells, c = act.shape
    block = block_of(n)
    shapes = [
        jax.ShapeDtypeStruct((n, cells, c), bf16),
        jax.ShapeDtypeStruct((n, h, wd, c), bf16),
        jax.ShapeDtypeStruct((n, 4, wd, c), bf16),
        jax.ShapeDtypeStruct(head_t.shape, f32),
    ]
    return pl.pallas_call(
        functools.partial(back_kernel, block, h, wd),
        grid=(n // block,),
        out_shape=shapes,
        in_specs=[
            tiles(block, slope_out.shape[1:]),
            tiles(block, (cells, c)),
            tiles(block, (cells, c)),
            whole(head_t.shape),
            layer(w.shape, 1),
        ],
        out_specs=[tiles(block, s.shape[1:]) for s in shapes[:3]] + [whole(head_t.shape)],
        scratch_shapes=[
            VMEM((3, c, 3 * c), bf16),
            VMEM((2, c, 3 * c), bf16),
            VMEM((h + 4, wd + 16, c), f32),
            VMEM((block, h + 4, wd, 3 * c), bf16),
            VMEM((2, block, h, 3 * c), bf16),
        ],
        compiler_params=pltpu.CompilerParams(vmem_limit_bytes=LIMIT),
        name="backward",
    )(slope_out, act, pre, head_t, w)


def grad_kernel(block, steps, mid, h, w, *refs):
    if mid:
        index_ref, flip_ref, edges_ref, inner_ref, pre_ref, x3_ref, out_ref, acc, field = refs
    else:
        slope_ref, x3_ref, out_ref, acc = refs
    c = out_ref.shape[-1]
    step = pl.program_id(0)

    @pl.when(step == 0)
    def _():
        acc[...] = jnp.zeros_like(acc)

    slopes = []
    for k in range(block):
        if mid:
            rims = rims_of(index_ref, flip_ref, edges_ref, step * block + k, w)
            field[...] = inner_ref[k].astype(f32)
            field[0] += rims[0:w]
            field[:, w - 1 : w, :] += rims[w : w + h].reshape(h, 1, c)
            field[h - 1] += rims[w + h : 2 * w + h]
            field[:, 0:1, :] += rims[2 * w + h :].reshape(h, 1, c)
            slope = (field[...].reshape(h * w, c) * dsilu(pre_ref[k])).astype(bf16)
        else:
            slope = slope_ref[k]
        slopes.append(slope.T)
    turned = jnp.concatenate(slopes, axis=1)
    for a in range(3):
        acc[a] += mm(turned, x3_ref[:, a : a + h].reshape(block * h * w, 3 * c))

    @pl.when(step == steps - 1)
    def _():
        for a in range(3):
            for b in range(3):
                out_ref[(3 * a + b) * c : (3 * a + b + 1) * c, :] = acc[
                    a, :, b * c : (b + 1) * c
                ].T


def weight_grad(x3, h, w, c, slope=None, mid=None):
    n = x3.shape[0]
    block = block_of(n)
    steps = n // block
    scratch = [VMEM((3, c, 3 * c), f32)]
    if mid is None:
        args = [slope, x3]
        in_specs = [tiles(block, slope.shape[1:]), tiles(block, x3.shape[1:])]
    else:
        index, flips, edges, inner, pre = mid
        args = [index, flips, edges, inner, pre, x3]
        in_specs = [
            SMEM_SPEC,
            SMEM_SPEC,
            whole(edges.shape),
            tiles(block, inner.shape[1:]),
            tiles(block, pre.shape[1:]),
            tiles(block, x3.shape[1:]),
        ]
        scratch.append(VMEM((h, w, c), f32))
    return pl.pallas_call(
        functools.partial(grad_kernel, block, steps, mid is not None, h, w),
        grid=(steps,),
        out_shape=jax.ShapeDtypeStruct((9 * c, c), f32),
        in_specs=in_specs,
        out_specs=whole((9 * c, c)),
        scratch_shapes=scratch,
        compiler_params=pltpu.CompilerParams(vmem_limit_bytes=LIMIT),
        name="grad_two" if mid is None else "grad_one",
    )(*args)


def shards(faces, zs, features, observed, conv_weights, head_weight, adjacency, placement_map):
    members, tile_dev, h, w, c = features.shape
    n = members * tile_dev
    variables = head_weight.shape[1]
    x = features.reshape(n, h, w, c)
    rows = conv_weights.shape[0]
    head_rows = head_weight.shape[0]
    lanes = -(-variables // 128) * 128
    head_wide = jnp.pad(head_weight, ((0, 0), (0, lanes - variables)))
    edges, weights, head = first_gather(
        x, [conv_weights.reshape(rows, 2 * c), head_wide], faces, zs
    )
    weights = weights.reshape(faces * zs * rows, 2 * c)
    head_t = head.reshape(faces * zs * head_rows, lanes)[:, :variables].T

    def flat(e):
        return e.reshape((faces * n * 4,) + e.shape[-2:])

    x3_one, pre_one, act_one, sides, index, flips = conv(
        (placement_map, adjacency.reshape(-1)), x, flat(edges), weights, members=members
    )
    x3_two, pre_two, act_two, outs = conv(
        (index, flips), act_one, flat(face_gather(sides, faces, 2)), weights, head_t=head_t
    )
    slope_out = score_exchange(outs, observed, zs, h, 3)
    slope_two, inner, borders, hg = backward(slope_out, act_two, pre_two, head_t, weights, h, w)
    grad_two = weight_grad(x3_two, h, w, c, slope=slope_two)
    returned = flat(face_gather(borders, faces, 4))
    grad_one = weight_grad(x3_one, h, w, c, mid=(index, flips, returned, inner, pre_one))
    hg = jnp.pad(hg.T, ((0, 0), (0, lanes - variables)))
    chips = faces // 2
    one, two, head_out = scatter(
        [
            grad_one.reshape(chips, 2, zs, rows, c),
            grad_two.reshape(chips, 2, zs, rows, c),
            hg.reshape(chips, 2, zs, head_rows, lanes),
        ],
        faces,
        zs,
        5,
    )
    return jnp.stack([one, two], axis=1), head_out[:, :variables]


def solution(mesh):
    in_specs = (
        P("member", "face", None, None, None),
        P("face", None, "member"),
        P(("face", "member"), None, None),
        P(("face", "member"), None),
        P(),
        P(),
    )
    out_specs = (P(("face", "member"), None, None), P(("face", "member"), None))
    body = functools.partial(shards, mesh.shape["face"], mesh.shape["member"])
    return jax.shard_map(body, mesh=mesh, in_specs=in_specs, out_specs=out_specs, check_vma=False)
```

```python
import functools

import jax
import jax.numpy as jnp
from jax import lax
from jax.experimental import pallas as pl
from jax.experimental.pallas import tpu as pltpu
from jax.sharding import PartitionSpec as P

smooth_sq = 0.0625
MESH = pl.DeviceIdType.MESH
VMEM = pltpu.VMEM
f32 = jnp.float32
bf16 = jnp.bfloat16
LIMIT = 60 * 1024 * 1024
NT = (((1,), (1,)), ((), ()))
TN = (((0,), (0,)), ((), ()))
NN = (((1,), (0,)), ((), ()))


def mm(a, b, dims=NN):
    return lax.dot_general(a, b, dims, preferred_element_type=f32)


def rcopy(src, dst, send, recv, **where):
    return pltpu.make_async_remote_copy(
        src_ref=src, dst_ref=dst, send_sem=send, recv_sem=recv, device_id=where, device_id_type=MESH
    )


def greet(chips, members, face_axis, member_axis):
    face = lax.axis_index("face")
    member = lax.axis_index("member")
    core = face % 2
    chip = face // 2
    barrier = pltpu.get_barrier_semaphore()
    count = 0
    if face_axis:
        pl.semaphore_signal(
            barrier, inc=1, device_id={"face": chip * 2 + 1 - core}, device_id_type=MESH
        )
        for j in range(1, chips):
            pl.semaphore_signal(
                barrier,
                inc=1,
                device_id={"face": ((chip + j) % chips) * 2 + core},
                device_id_type=MESH,
            )
        count += chips
    if member_axis:
        for j in range(1, members):
            pl.semaphore_signal(
                barrier, inc=1, device_id={"member": (member + j) % members}, device_id_type=MESH
            )
        count += members - 1
    pl.semaphore_wait(barrier, count)


def line_gather(x_ref, out_at, member, members, sems):
    ups, upr, dns, dnr = sems
    steps = members - 1

    def up(s):
        b = jnp.maximum(member - s, 0)
        return rcopy(
            x_ref if s == 0 else out_at(b),
            out_at(b),
            ups.at[s],
            upr.at[s],
            member=jnp.minimum(member + 1, members - 1),
        )

    def down(s):
        b = jnp.minimum(member + s, members - 1)
        return rcopy(
            x_ref if s == 0 else out_at(b),
            out_at(b),
            dns.at[s],
            dnr.at[s],
            member=jnp.maximum(member - 1, 0),
        )

    def up_goes(s):
        return jnp.logical_and(member - s >= 0, member < members - 1)

    def down_goes(s):
        return jnp.logical_and(member + s < members, member > 0)

    pl.when(up_goes(0))(lambda: up(0).start())
    pl.when(down_goes(0))(lambda: down(0).start())
    for s in range(steps):
        pl.when(member - 1 - s >= 0)(lambda: up(s).wait_recv())
        if s + 1 < steps:
            pl.when(up_goes(s + 1))(lambda: up(s + 1).start())
        pl.when(member + 1 + s < members)(lambda: down(s).wait_recv())
        if s + 1 < steps:
            pl.when(down_goes(s + 1))(lambda: down(s + 1).start())
    for s in range(steps):
        pl.when(up_goes(s))(lambda: up(s).wait_send())
        pl.when(down_goes(s))(lambda: down(s).wait_send())


class FaceGather:
    def __init__(self, src, out, chips, sems):
        self.src, self.out, self.chips = src, out, chips
        self.send, self.recv, self.fsend, self.frecv = sems
        face = lax.axis_index("face")
        self.face, self.core, self.chip = face, face % 2, face // 2
        self.partner = self.chip * 2 + 1 - self.core

    def direct(self, j):
        return rcopy(
            self.src,
            self.out.at[self.face],
            self.send.at[j],
            self.recv.at[j],
            face=((self.chip + j) % self.chips) * 2 + self.core,
        )

    def forward(self, j):
        block = ((self.chip + self.chips - j) % self.chips) * 2 + self.core
        return rcopy(
            self.src if j == 0 else self.out.at[block],
            self.out.at[block],
            self.fsend.at[j],
            self.frecv.at[j],
            face=self.partner,
        )

    def start(self):
        for j in range(1, self.chips):
            self.direct(j).start()
        self.forward(0).start()

    def relay(self):
        self.relay_first()
        self.relay_rest()

    def relay_first(self):
        pass

    def relay_rest(self):
        for j in range(1, self.chips):
            self.direct(j).wait_recv()
            self.forward(j).start()

    def finish(self):
        for j in range(1, self.chips):
            self.direct(j).wait_send()
        for j in range(self.chips):
            self.forward(j).wait()


class SquareGather:
    def __init__(self, src, out, chips, sems):
        self.src, self.out = src, out
        self.send, self.recv, self.fsend, self.frecv = sems
        face = lax.axis_index("face")
        core, chip = face % 2, face // 2
        col, row = chip % 2, chip // 2
        self.face = face
        self.partner = chip * 2 + 1 - core
        self.beside = (row * 2 + 1 - col) * 2 + core
        self.below = ((1 - row) * 2 + col) * 2 + core
        self.across = ((1 - row) * 2 + 1 - col) * 2 + core
        self.half = src.shape[0] // 2

    def part(self, k):
        return pl.ds((0, 1, 1, 0, 0, 1)[k] * self.half, self.half)

    def came(self, k):
        block = (self.beside, self.beside, self.below, self.below, self.across, self.across)[k]
        return self.out.at[block, self.part(k)]

    def direct(self, k):
        to = (self.beside, self.beside, self.below, self.below, self.below, self.beside)[k]
        if k < 4:
            src, block = self.src.at[self.part(k)], self.face
        else:
            block = self.beside if k == 4 else self.below
            src = self.out.at[block, self.part(k)]
        return rcopy(
            src, self.out.at[block, self.part(k)], self.send.at[k], self.recv.at[k], face=to
        )

    def forward(self, k):
        if k == 6:
            src, dst = self.src, self.out.at[self.face]
        else:
            src = dst = self.came(k)
        return rcopy(src, dst, self.fsend.at[k], self.frecv.at[k], face=self.partner)

    def start(self):
        for k in (0, 2, 1, 3):
            self.direct(k).start()
        self.forward(6).start()

    def relay(self):
        self.relay_first()
        self.relay_rest()

    def relay_first(self):
        for k, onward in ((0, 4), (2, 5)):
            self.direct(k).wait_recv()
            self.direct(onward).start()
            self.forward(k).start()

    def relay_rest(self):
        for k in (1, 3, 4, 5):
            self.direct(k).wait_recv()
            self.forward(k).start()

    def finish(self):
        for k in range(6):
            self.direct(k).wait_send()
        for k in range(7):
            self.forward(k).wait()


def gather_over_face(src, out, chips, sems):
    kind = SquareGather if chips == 4 and src.shape[0] % 2 == 0 else FaceGather
    return kind(src, out, chips, sems)


def dma_sems(*sizes):
    return [pltpu.SemaphoreType.DMA((max(n, 1),)) for n in sizes]


def first_gather_kernel(chips, members, count, *refs):
    x, ws = refs[0], refs[1 : 1 + count]
    edges_out, outs = refs[1 + count], refs[2 + count : 2 + 2 * count]
    edges, field, own_sem = refs[2 + 2 * count : 5 + 2 * count]
    sems = refs[5 + 2 * count :]
    face = lax.axis_index("face")
    member = lax.axis_index("member")
    own = []
    for k in range(count):
        own.append(
            pltpu.make_async_copy(ws[k], outs[k].at[face, member], own_sem.at[k + 1])
        )
        own[k].start()

    def cut(k, carry):
        field[...] = x[k].astype(f32)
        sides_out(field, edges, k)
        return carry

    lax.fori_loop(0, x.shape[0], cut, 0)
    greet(chips, members, True, True)
    eg = gather_over_face(edges, edges_out, chips, sems[:4])
    eg.start()
    edges_out[face] = edges[...]
    for c in own:
        c.wait()
    rest = sems[4:]
    wgs = []
    for k in range(count):
        line = rest[8 * k : 8 * k + 4]
        line_gather(ws[k], lambda b: outs[k].at[face, b], member, members, line)
        wg = gather_over_face(outs[k].at[face], outs[k], chips, rest[8 * k + 4 : 8 * k + 8])
        wg.start()
        wgs.append(wg)
        if k == 0:
            eg.relay_first()
    eg.relay_rest()
    for wg in wgs:
        wg.relay()
    eg.finish()
    for wg in wgs:
        wg.finish()


def first_gather(x, ws, faces, members):
    chips = faces // 2
    count = len(ws)
    n, h, w, c = x.shape
    shapes = [jax.ShapeDtypeStruct((faces, n, 4, w, c), x.dtype)] + [
        jax.ShapeDtypeStruct((faces, members) + v.shape, v.dtype) for v in ws
    ]
    scratch = [VMEM((n, 4, w, c), x.dtype), VMEM((h, w, c), f32)]
    scratch += dma_sems(count + 1) + dma_sems(*([chips + 3] * 4))
    for _ in ws:
        scratch += dma_sems(*([members] * 4)) + dma_sems(*([chips + 3] * 4))
    return pl.pallas_call(
        functools.partial(first_gather_kernel, chips, members, count),
        out_shape=shapes,
        in_specs=[pl.BlockSpec(memory_space=VMEM)] * (count + 1),
        out_specs=[pl.BlockSpec(memory_space=VMEM)] * (count + 1),
        scratch_shapes=scratch,
        compiler_params=pltpu.CompilerParams(
            collective_id=1, has_side_effects=True, vmem_limit_bytes=LIMIT
        ),
        name="first_gather",
    )(x, *ws)


def face_gather_kernel(chips, x, out, own_sem, *sems):
    own = pltpu.make_async_copy(x, out.at[lax.axis_index("face")], own_sem.at[0])
    own.start()
    greet(chips, 1, True, False)
    g = gather_over_face(x, out, chips, sems)
    g.start()
    own.wait()
    g.relay()
    g.finish()


def face_gather(x, faces, ident):
    chips = faces // 2
    return pl.pallas_call(
        functools.partial(face_gather_kernel, chips),
        out_shape=jax.ShapeDtypeStruct((faces,) + x.shape, x.dtype),
        in_specs=[pl.BlockSpec(memory_space=VMEM)],
        out_specs=pl.BlockSpec(memory_space=VMEM),
        scratch_shapes=dma_sems(1) + dma_sems(*([chips + 3] * 4)),
        compiler_params=pltpu.CompilerParams(
            collective_id=ident, has_side_effects=True, vmem_limit_bytes=LIMIT
        ),
        name="face_gather",
    )(x)


def score_kernel(members, held, tile_dev, chunk, h, *refs):
    y, obs, out, packed, came, slopes, back = refs[:7]
    s1, r1, s2, r2 = refs[7:]
    member = lax.axis_index("member")
    part = obs.shape[-1]
    ensemble = held * members
    chunks = tile_dev // chunk

    def there(j):
        return (member + j) % members

    def source(j):
        return (member + members - j) % members

    def go(i, j):
        at = pl.ds(i * chunk, chunk)
        return rcopy(
            packed.at[there(j), at], came.at[j, at], s1.at[i, j], r1.at[i, j], member=there(j)
        )

    def home(i, j):
        at = pl.ds(i * chunk, chunk)
        return rcopy(
            slopes.at[j, at], back.at[member, at], s2.at[i, j], r2.at[i, j], member=source(j)
        )

    def home_here(i, j):
        at = pl.ds(i * chunk, chunk)
        return rcopy(
            slopes.at[j, at], back.at[there(j), at], s2.at[i, j], r2.at[i, j], member=source(j)
        )

    def pack(t):
        for q in range(members):
            packed[q, t] = jnp.concatenate(
                [y[m * tile_dev + t][:, q * part : (q + 1) * part] for m in range(held)], axis=1
            )

    def g(v):
        return v * lax.rsqrt(v * v + smooth_sq)

    def score(t):
        o = obs[t].astype(f32)
        o = jnp.concatenate([o] * held, axis=1)
        vals = [packed[member, t].astype(f32)]
        vals += [came[j, t].astype(f32) for j in range(1, members)]
        turned = [
            jnp.concatenate([v[:, k * part :], v[:, : k * part]], axis=1) if k else v
            for v in vals
            for k in range(held)
        ]
        for j in range(members):
            v = vals[j]
            paired = jnp.zeros_like(v)
            for u in turned:
                paired = paired + g(v - u)
            s = (g(v - o) / ensemble - paired / (ensemble * ensemble)) / h
            s = s.astype(bf16)
            if j == 0:
                back[member, t] = s
            else:
                slopes[j, t] = s

    pack_first = [pack(t) for t in range(chunk)]
    del pack_first
    greet(1, members, False, True)
    for i in range(chunks):
        if i:
            for t in range(i * chunk, (i + 1) * chunk):
                pack(t)
        for j in range(1, members):
            go(i, j).start()
    for i in range(chunks):
        for j in range(1, members):
            go(i, j).wait_recv()
        for t in range(i * chunk, (i + 1) * chunk):
            score(t)
        for j in range(1, members):
            home(i, j).start()
    for i in range(chunks):
        for j in range(1, members):
            home_here(i, j).wait_recv()
        for t in range(i * chunk, (i + 1) * chunk):
            for m in range(held):
                out[m * tile_dev + t] = jnp.concatenate(
                    [back[q, t][:, m * part : (m + 1) * part] for q in range(members)], axis=1
                )
    for i in range(chunks):
        for j in range(1, members):
            go(i, j).wait_send()
            home(i, j).wait_send()


def score_exchange(y, obs, members, h, ident):
    n, variables, cells = y.shape
    tile_dev = obs.shape[0]
    held = n // tile_dev
    chunk = 2 if tile_dev % 2 == 0 else 1
    wide = (members, tile_dev, variables, held * obs.shape[-1])
    sems = pltpu.SemaphoreType.DMA((tile_dev // chunk, members))
    return pl.pallas_call(
        functools.partial(score_kernel, members, held, tile_dev, chunk, h),
        out_shape=jax.ShapeDtypeStruct(y.shape, bf16),
        in_specs=[pl.BlockSpec(memory_space=VMEM)] * 2,
        out_specs=pl.BlockSpec(memory_space=VMEM),
        scratch_shapes=[VMEM(wide, bf16)] * 4 + [sems] * 4,
        compiler_params=pltpu.CompilerParams(
            collective_id=ident, has_side_effects=True, vmem_limit_bytes=LIMIT
        ),
        name="score",
    )(y, obs)


class Scatter:
    def __init__(self, g, out, chips, members, scratch):
        self.g, self.out, self.chips, self.members = g, out, chips, members
        self.fromcore, self.acc, self.fromchip, self.fromline = scratch[:4]
        self.s0, self.r0, self.s1, self.r1, self.s2, self.r2 = scratch[4:]
        face = lax.axis_index("face")
        self.member = lax.axis_index("member")
        self.core, self.chip = face % 2, face // 2
        self.partner = self.chip * 2 + 1 - self.core
        self.order = list(range(1, chips)) + [0]

    def there(self, j):
        return (self.chip + j) % self.chips

    def core_copy(self, j):
        return rcopy(
            self.g.at[self.there(j), 1 - self.core],
            self.fromcore.at[j],
            self.s0.at[j],
            self.r0.at[j],
            face=self.partner,
        )

    def chip_copy(self, j):
        return rcopy(
            self.acc.at[j],
            self.fromchip.at[j],
            self.s1.at[j],
            self.r1.at[j],
            face=self.there(j) * 2 + self.core,
        )

    def line_copy(self, j):
        to = (self.member + j) % self.members
        return rcopy(
            self.acc.at[0, to], self.fromline.at[j], self.s2.at[j], self.r2.at[j], member=to
        )

    def core_start(self):
        for j in self.order:
            self.core_copy(j).start()

    def core_done(self):
        for j in self.order:
            self.core_copy(j).wait_recv()
            self.acc[j] = self.g[self.there(j), self.core] + self.fromcore[j]
            if j:
                self.chip_copy(j).start()

    def chip_done(self):
        for j in range(1, self.chips):
            self.chip_copy(j).wait_recv()
            self.acc[0] = self.acc[0] + self.fromchip[j]
        for j in range(1, self.members):
            self.line_copy(j).start()

    def line_done(self):
        total = self.acc[0, self.member]
        for j in range(1, self.members):
            self.line_copy(j).wait_recv()
            total = total + self.fromline[j]
        self.out[...] = total

    def finish(self):
        for j in range(self.chips):
            self.core_copy(j).wait_send()
        for j in range(1, self.chips):
            self.chip_copy(j).wait_send()
        for j in range(1, self.members):
            self.line_copy(j).wait_send()


def scatter_scratch(chips, members, tail):
    return [
        VMEM((chips, members) + tail, f32),
        VMEM((chips, members) + tail, f32),
        VMEM((chips, members) + tail, f32),
        VMEM((members,) + tail, f32),
    ] + dma_sems(chips, chips, chips, chips, members, members)


def rims_of(index_ref, flip_ref, edges_ref, n, length):
    cat = jnp.concatenate([edges_ref[index_ref[n * 4 + a]] for a in range(4)], axis=0)
    size = 4 * length
    row = lax.broadcasted_iota(jnp.int32, (size, size), 0)
    col = lax.broadcasted_iota(jnp.int32, (size, size), 1)
    side = row // length
    place = row - side * length
    flag = jnp.zeros((size, size), jnp.int32)
    for a in range(4):
        flag = jnp.where(side == a, flip_ref[n * 4 + a], flag)
    target = side * length + jnp.where(flag == 1, length - 1 - place, place)
    return mm(jnp.where(col == target, 1.0, 0.0).astype(bf16), cat)


def col_to_rows(ref_slice):
    height, _, channels = ref_slice.shape
    return ref_slice.reshape(height, channels)


def sides_out(field, edge_ref, k):
    w = field.shape[1]
    h = field.shape[0]
    edge_ref[k, 0] = field[0].astype(bf16)
    edge_ref[k, 1] = col_to_rows(field[:, w - 1 : w, :]).astype(bf16)
    edge_ref[k, 2] = field[h - 1].astype(bf16)
    edge_ref[k, 3] = col_to_rows(field[:, 0:1, :]).astype(bf16)


def silu(v):
    return v / (1.0 + jnp.exp(-v))


def dsilu(v):
    s = 1.0 / (1.0 + jnp.exp(-v))
    return s * (1.0 + v * (1.0 - s))


def table(place_ref, glue_ref, index_ref, flip_ref, slot_of, members, tile_dev):
    first = lax.axis_index("face") * tile_dev

    def invert(s, carry):
        slot_of[place_ref[s]] = s
        return carry

    lax.fori_loop(0, place_ref.shape[0], invert, 0)

    def fill(i, carry):
        tile = place_ref[first + i]
        for a in range(4):
            base = (tile * 4 + a) * 3
            slot = slot_of[glue_ref[base]]
            face = slot // tile_dev
            inner = slot - face * tile_dev
            for m in range(members):
                at = (m * tile_dev + i) * 4 + a
                index_ref[at] = ((face * members + m) * tile_dev + inner) * 4 + glue_ref[base + 1]
                flip_ref[at] = glue_ref[base + 2]
        return carry

    lax.fori_loop(0, tile_dev, fill, 0)


def conv_kernel(block, members, *refs):
    last = members is None
    if last:
        index_ref, flip_ref, x_ref, edges_ref, w_ref = refs[:5]
        head_ref, x3_ref, pre_ref, act_ref, out_ref, pad = refs[5:]
    else:
        place_ref, glue_ref, x_ref, edges_ref, w_ref = refs[:5]
        x3_ref, pre_ref, act_ref, side_ref, index_ref, flip_ref, pad, field, slot_of = refs[5:]
    _, h, w, c = x_ref.shape
    step = pl.program_id(0)
    if not last:
        tile_dev = index_ref.shape[0] // (4 * members)
        pl.when(step == 0)(
            lambda: table(place_ref, glue_ref, index_ref, flip_ref, slot_of, members, tile_dev)
        )
    for k in range(block):
        n = step * block + k
        rims = rims_of(index_ref, flip_ref, edges_ref, n, w)
        zero = jnp.zeros((8, c), f32)
        for r in (0, h + 1):
            pad[r, 0:8, :] = zero
            pad[r, 8 + w : 16 + w, :] = zero
        pad[1 : h + 1, 8 : 8 + w, :] = x_ref[k].astype(f32)
        pad[0, 8 : 8 + w, :] = rims[0:w]
        pad[1 : h + 1, 8 + w : 9 + w, :] = rims[w : w + h].reshape(h, 1, c)
        pad[h + 1, 8 : 8 + w, :] = rims[w + h : 2 * w + h]
        pad[1 : h + 1, 7:8, :] = rims[2 * w + h :].reshape(h, 1, c)
        for b in range(3):
            x3_ref[k, :, :, b * c : (b + 1) * c] = pad[:, 7 + b : 7 + b + w, :].astype(bf16)
    pre = None
    for a in range(3):
        part = mm(
            x3_ref[:, a : a + h].reshape(block * h * w, 3 * c),
            w_ref[3 * a * c : 3 * (a + 1) * c, :],
        )
        pre = part if pre is None else pre + part
    pre_ref[...] = pre.reshape(block, h * w, c)
    act = silu(pre).astype(bf16)
    act_ref[...] = act.reshape(act_ref.shape)
    if last:
        for k in range(block):
            out_ref[k] = mm(head_ref[...], act[k * h * w : (k + 1) * h * w], NT).astype(bf16)
    else:
        for k in range(block):
            field[...] = act[k * h * w : (k + 1) * h * w].astype(f32).reshape(h, w, c)
            sides_out(field, side_ref, k)


def whole(shape):
    return pl.BlockSpec(shape, lambda i: (0,) * len(shape))


def tiles(block, shape):
    return pl.BlockSpec((block,) + shape, lambda i: (i,) + (0,) * len(shape))


SMEM_SPEC = pl.BlockSpec(memory_space=pltpu.SMEM)


def block_of(n):
    return 3 if n % 3 == 0 else (2 if n % 2 == 0 else 1)


def layer(shape, which):
    return pl.BlockSpec((shape[0], shape[1] // 2), lambda i: (0, which))


def conv(scalars, x, edges, w, members=None, head_t=None):
    n, h, wd, c = x.shape
    block = block_of(n)
    last = members is None
    in_specs = [
        SMEM_SPEC,
        SMEM_SPEC,
        tiles(block, (h, wd, c)),
        whole(edges.shape),
        layer(w.shape, int(last)),
    ]
    shapes = [
        jax.ShapeDtypeStruct((n, h + 2, wd, 3 * c), bf16),
        jax.ShapeDtypeStruct((n, h * wd, c), f32),
        jax.ShapeDtypeStruct((n, h * wd, c) if last else (n, h, wd, c), bf16),
    ]
    args = [*scalars, x, edges, w]
    scratch = [VMEM((h + 2, wd + 16, c), f32)]
    if last:
        in_specs.append(whole(head_t.shape))
        args.append(head_t)
        shapes.append(jax.ShapeDtypeStruct((n, head_t.shape[0], h * wd), bf16))
    else:
        shapes.append(jax.ShapeDtypeStruct((n, 4, wd, c), bf16))
        scratch.append(VMEM((h, wd, c), f32))
        scratch.append(pltpu.SMEM(scalars[0].shape, jnp.int32))
    out_specs = [tiles(block, s.shape[1:]) for s in shapes]
    if not last:
        shapes += [jax.ShapeDtypeStruct((n * 4,), jnp.int32)] * 2
        out_specs += [SMEM_SPEC] * 2
    return pl.pallas_call(
        functools.partial(conv_kernel, block, members),
        grid=(n // block,),
        out_shape=shapes,
        in_specs=in_specs,
        out_specs=out_specs,
        scratch_shapes=scratch,
        compiler_params=pltpu.CompilerParams(vmem_limit_bytes=LIMIT),
        name="conv_last" if last else "conv_first",
    )(*args)


def back_kernel(block, h, w, *refs):
    out_ref, act_ref, pre_ref, head_ref, w_ref = refs[:5]
    slope_ref, inner_ref, side_ref, hg_ref, va, vb, pad, s3, cols = refs[5:]
    c = act_ref.shape[-1]
    step = pl.program_id(0)

    @pl.when(step == 0)
    def _():
        hg_ref[...] = jnp.zeros_like(hg_ref)
        for a in range(3):
            for b in range(3):
                tap = w_ref[(3 * a + b) * c : (3 * a + b + 1) * c, :]
                va[a, :, b * c : (b + 1) * c] = tap
                if b == 0:
                    vb[0, :, a * c : (a + 1) * c] = tap
                if b == 2:
                    vb[1, :, a * c : (a + 1) * c] = tap
        pad[...] = jnp.zeros_like(pad)

    for k in range(block):
        slope_out = out_ref[k]
        hg_ref[...] += mm(slope_out, act_ref[k])
        back = mm(slope_out, head_ref[...], TN)
        slope = (back * dsilu(pre_ref[k])).astype(bf16)
        slope_ref[k] = slope
        pad[2 : h + 2, 8 : 8 + w, :] = slope.astype(f32).reshape(h, w, c)
        for b in range(3):
            s3[k, :, :, b * c : (b + 1) * c] = pad[:, 9 - b : 9 - b + w, :].astype(bf16)
        left = pad[:, 8:9, :].reshape(h + 4, c)
        right = pad[:, 7 + w : 8 + w, :].reshape(h + 4, c)
        for a in range(3):
            cols[0, k, :, a * c : (a + 1) * c] = left[3 - a : 3 - a + h].astype(bf16)
            cols[1, k, :, a * c : (a + 1) * c] = right[3 - a : 3 - a + h].astype(bf16)
    full = None
    for a in range(3):
        part = mm(s3[:, 2 - a : 20 - a + h - 16].reshape(block * (h + 2) * w, 3 * c), va[a], NT)
        full = part if full is None else full + part
    full = full.reshape(block, h + 2, w, c).astype(bf16)
    inner_ref[...] = full[:, 1 : h + 1]
    lefts = mm(cols[0].reshape(block * h, 3 * c), vb[0], NT).astype(bf16)
    rights = mm(cols[1].reshape(block * h, 3 * c), vb[1], NT).astype(bf16)
    for k in range(block):
        side_ref[k, 0] = full[k, 0]
        side_ref[k, 1] = rights[k * h : (k + 1) * h]
        side_ref[k, 2] = full[k, h + 1]
        side_ref[k, 3] = lefts[k * h : (k + 1) * h]


def backward(slope_out, act, pre, head_t, w, h, wd):
    n, cells, c = act.shape
    block = block_of(n)
    shapes = [
        jax.ShapeDtypeStruct((n, cells, c), bf16),
        jax.ShapeDtypeStruct((n, h, wd, c), bf16),
        jax.ShapeDtypeStruct((n, 4, wd, c), bf16),
        jax.ShapeDtypeStruct(head_t.shape, f32),
    ]
    return pl.pallas_call(
        functools.partial(back_kernel, block, h, wd),
        grid=(n // block,),
        out_shape=shapes,
        in_specs=[
            tiles(block, slope_out.shape[1:]),
            tiles(block, (cells, c)),
            tiles(block, (cells, c)),
            whole(head_t.shape),
            layer(w.shape, 1),
        ],
        out_specs=[tiles(block, s.shape[1:]) for s in shapes[:3]] + [whole(head_t.shape)],
        scratch_shapes=[
            VMEM((3, c, 3 * c), bf16),
            VMEM((2, c, 3 * c), bf16),
            VMEM((h + 4, wd + 16, c), f32),
            VMEM((block, h + 4, wd, 3 * c), bf16),
            VMEM((2, block, h, 3 * c), bf16),
        ],
        compiler_params=pltpu.CompilerParams(vmem_limit_bytes=LIMIT),
        name="backward",
    )(slope_out, act, pre, head_t, w)


def add_products(acc, slopes, x3_ref, h, w):
    block, _, _, width = x3_ref.shape
    turned = jnp.concatenate([v.T for v in slopes], axis=1)
    for a in range(3):
        acc[a] += mm(turned, x3_ref[:, a : a + h].reshape(block * h * w, width))


def turn_out(acc, out_ref):
    c = out_ref.shape[-1]
    for a in range(3):
        for b in range(3):
            out_ref[(3 * a + b) * c : (3 * a + b + 1) * c, :] = acc[
                a, :, b * c : (b + 1) * c
            ].T


def grad_two_kernel(block, steps, chips, h, w, *refs):
    slope_ref, x3_ref, side_ref, out_ref, sides_ref, acc, own_sem = refs[:7]
    step = pl.program_id(0)
    gather = gather_over_face(side_ref, sides_ref, chips, refs[7:])
    own = pltpu.make_async_copy(side_ref, sides_ref.at[lax.axis_index("face")], own_sem.at[0])

    @pl.when(step == 0)
    def _():
        own.start()
        greet(chips, 1, True, False)
        gather.start()
        acc[...] = jnp.zeros_like(acc)

    add_products(acc, [slope_ref[k] for k in range(block)], x3_ref, h, w)

    @pl.when(step == min(1, steps - 1))
    def _():
        gather.relay_first()

    @pl.when(step == steps - 1)
    def _():
        turn_out(acc, out_ref)
        own.wait()
        gather.relay_rest()
        gather.finish()


def grad_two_gather(x3, slope, sides, h, w, faces, ident):
    n, _, _, width = x3.shape
    c = width // 3
    block = block_of(n)
    chips = faces // 2
    return pl.pallas_call(
        functools.partial(grad_two_kernel, block, n // block, chips, h, w),
        grid=(n // block,),
        out_shape=[
            jax.ShapeDtypeStruct((9 * c, c), f32),
            jax.ShapeDtypeStruct((faces,) + sides.shape, sides.dtype),
        ],
        in_specs=[
            tiles(block, slope.shape[1:]),
            tiles(block, x3.shape[1:]),
            whole(sides.shape),
        ],
        out_specs=[whole((9 * c, c)), pl.BlockSpec(memory_space=pl.ANY)],
        scratch_shapes=[VMEM((3, c, width), f32)]
        + dma_sems(1)
        + dma_sems(*([chips + 3] * 4)),
        compiler_params=pltpu.CompilerParams(
            collective_id=ident, has_side_effects=True, vmem_limit_bytes=LIMIT
        ),
        name="grad_two",
    )(slope, x3, sides)


def grad_one_kernel(block, steps, chips, members, h, w, *refs):
    index_ref, flip_ref, edges_ref, inner_ref, pre_ref, x3_ref, two_ref, hg_ref = refs[:8]
    one_out, two_out, hg_out, acc, field, one_flat, one = refs[8:15]
    rest = refs[15:]
    c = one_flat.shape[-1]
    step = pl.program_id(0)
    s_two = Scatter(two_ref, two_out, chips, members, rest[:10])
    s_head = Scatter(hg_ref, hg_out, chips, members, rest[10:20])
    s_one = Scatter(one, one_out, chips, members, rest[20:30])

    @pl.when(step == 0)
    def _():
        greet(chips, members, True, True)
        s_two.core_start()
        s_head.core_start()
        acc[...] = jnp.zeros_like(acc)

    slopes = []
    for k in range(block):
        rims = rims_of(index_ref, flip_ref, edges_ref, step * block + k, w)
        field[...] = inner_ref[k].astype(f32)
        field[0] += rims[0:w]
        field[:, w - 1 : w, :] += rims[w : w + h].reshape(h, 1, c)
        field[h - 1] += rims[w + h : 2 * w + h]
        field[:, 0:1, :] += rims[2 * w + h :].reshape(h, 1, c)
        slopes.append((field[...].reshape(h * w, c) * dsilu(pre_ref[k])).astype(bf16))
    add_products(acc, slopes, x3_ref, h, w)

    @pl.when(step == 0)
    def _():
        s_two.core_done()
        s_head.core_done()

    @pl.when(step == steps - 1)
    def _():
        turn_out(acc, one_flat)
        rows = one.shape[3]
        for d in range(chips * 2 * members):
            one[d // (2 * members), d // members % 2, d % members] = one_flat[
                d * rows : (d + 1) * rows
            ]
        s_one.core_start()
        s_one.core_done()
        s_two.chip_done()
        s_head.chip_done()
        s_one.chip_done()
        s_two.line_done()
        s_head.line_done()
        s_one.line_done()
        for s in (s_two, s_head, s_one):
            s.finish()


def grad_one_scatter(scalars, edges, inner, pre, x3, two, hg, faces, members, ident):
    n, h, w, c = inner.shape
    block = block_of(n)
    chips = faces // 2
    tails = [two.shape[3:], hg.shape[3:], two.shape[3:]]
    scratch = [
        VMEM((3, c, 3 * c), f32),
        VMEM((h, w, c), f32),
        VMEM((9 * c, c), f32),
        VMEM(two.shape, f32),
    ]
    for tail in tails:
        scratch += scatter_scratch(chips, members, tail)
    return pl.pallas_call(
        functools.partial(grad_one_kernel, block, n // block, chips, members, h, w),
        grid=(n // block,),
        out_shape=[jax.ShapeDtypeStruct(tails[k], f32) for k in (2, 0, 1)],
        in_specs=[
            SMEM_SPEC,
            SMEM_SPEC,
            whole(edges.shape),
            tiles(block, inner.shape[1:]),
            tiles(block, pre.shape[1:]),
            tiles(block, x3.shape[1:]),
            whole(two.shape),
            whole(hg.shape),
        ],
        out_specs=[whole(tails[k]) for k in (2, 0, 1)],
        scratch_shapes=scratch,
        compiler_params=pltpu.CompilerParams(
            collective_id=ident, has_side_effects=True, vmem_limit_bytes=LIMIT
        ),
        name="grad_one",
    )(*scalars, edges, inner, pre, x3, two, hg)


def shards(faces, zs, features, observed, conv_weights, head_weight, adjacency, placement_map):
    members, tile_dev, h, w, c = features.shape
    n = members * tile_dev
    variables = head_weight.shape[1]
    x = features.reshape(n, h, w, c)
    rows = conv_weights.shape[0]
    head_rows = head_weight.shape[0]
    lanes = -(-variables // 128) * 128
    head_wide = jnp.pad(head_weight, ((0, 0), (0, lanes - variables)))
    edges, weights, head = first_gather(
        x, [conv_weights.reshape(rows, 2 * c), head_wide], faces, zs
    )
    weights = weights.reshape(faces * zs * rows, 2 * c)
    head_t = head.reshape(faces * zs * head_rows, lanes)[:, :variables].T

    def flat(e):
        return e.reshape((faces * n * 4,) + e.shape[-2:])

    x3_one, pre_one, act_one, sides, index, flips = conv(
        (placement_map, adjacency.reshape(-1)), x, flat(edges), weights, members=members
    )
    x3_two, pre_two, act_two, outs = conv(
        (index, flips), act_one, flat(face_gather(sides, faces, 2)), weights, head_t=head_t
    )
    slope_out = score_exchange(outs, observed, zs, h, 3)
    slope_two, inner, borders, hg = backward(slope_out, act_two, pre_two, head_t, weights, h, w)
    grad_two, returned = grad_two_gather(x3_two, slope_two, borders, h, w, faces, 4)
    hg = jnp.pad(hg.T, ((0, 0), (0, lanes - variables)))
    chips = faces // 2
    one, two, head_out = grad_one_scatter(
        (index, flips),
        flat(returned),
        inner,
        pre_one,
        x3_one,
        grad_two.reshape(chips, 2, zs, rows, c),
        hg.reshape(chips, 2, zs, head_rows, lanes),
        faces,
        zs,
        5,
    )
    return jnp.stack([one, two], axis=1), head_out[:, :variables]


def solution(mesh):
    in_specs = (
        P("member", "face", None, None, None),
        P("face", None, "member"),
        P(("face", "member"), None, None),
        P(("face", "member"), None),
        P(),
        P(),
    )
    out_specs = (P(("face", "member"), None, None), P(("face", "member"), None))
    body = functools.partial(shards, mesh.shape["face"], mesh.shape["member"])
    return jax.shard_map(body, mesh=mesh, in_specs=in_specs, out_specs=out_specs, check_vma=False)
```

```python
import functools

import jax
import jax.numpy as jnp
from jax import lax
from jax.experimental import pallas as pl
from jax.experimental.pallas import tpu as pltpu
from jax.sharding import PartitionSpec as P

smooth_sq = 0.0625
MESH = pl.DeviceIdType.MESH
VMEM = pltpu.VMEM
f32 = jnp.float32
bf16 = jnp.bfloat16
LIMIT = 60 * 1024 * 1024
NT = (((1,), (1,)), ((), ()))
TN = (((0,), (0,)), ((), ()))
NN = (((1,), (0,)), ((), ()))


def mm(a, b, dims=NN):
    return lax.dot_general(a, b, dims, preferred_element_type=f32)


def rcopy(src, dst, send, recv, **where):
    return pltpu.make_async_remote_copy(
        src_ref=src, dst_ref=dst, send_sem=send, recv_sem=recv, device_id=where, device_id_type=MESH
    )


def greet(chips, members, face_axis, member_axis):
    face = lax.axis_index("face")
    member = lax.axis_index("member")
    core = face % 2
    chip = face // 2
    barrier = pltpu.get_barrier_semaphore()
    count = 0
    if face_axis:
        pl.semaphore_signal(
            barrier, inc=1, device_id={"face": chip * 2 + 1 - core}, device_id_type=MESH
        )
        for j in range(1, chips):
            pl.semaphore_signal(
                barrier,
                inc=1,
                device_id={"face": ((chip + j) % chips) * 2 + core},
                device_id_type=MESH,
            )
        count += chips
    if member_axis:
        for j in range(1, members):
            pl.semaphore_signal(
                barrier, inc=1, device_id={"member": (member + j) % members}, device_id_type=MESH
            )
        count += members - 1
    pl.semaphore_wait(barrier, count)


def line_gather(x_ref, out_at, member, members, sems):
    ups, upr, dns, dnr = sems
    steps = members - 1

    def up(s):
        b = jnp.maximum(member - s, 0)
        return rcopy(
            x_ref if s == 0 else out_at(b),
            out_at(b),
            ups.at[s],
            upr.at[s],
            member=jnp.minimum(member + 1, members - 1),
        )

    def down(s):
        b = jnp.minimum(member + s, members - 1)
        return rcopy(
            x_ref if s == 0 else out_at(b),
            out_at(b),
            dns.at[s],
            dnr.at[s],
            member=jnp.maximum(member - 1, 0),
        )

    def up_goes(s):
        return jnp.logical_and(member - s >= 0, member < members - 1)

    def down_goes(s):
        return jnp.logical_and(member + s < members, member > 0)

    pl.when(up_goes(0))(lambda: up(0).start())
    pl.when(down_goes(0))(lambda: down(0).start())
    for s in range(steps):
        pl.when(member - 1 - s >= 0)(lambda: up(s).wait_recv())
        if s + 1 < steps:
            pl.when(up_goes(s + 1))(lambda: up(s + 1).start())
        pl.when(member + 1 + s < members)(lambda: down(s).wait_recv())
        if s + 1 < steps:
            pl.when(down_goes(s + 1))(lambda: down(s + 1).start())
    for s in range(steps):
        pl.when(up_goes(s))(lambda: up(s).wait_send())
        pl.when(down_goes(s))(lambda: down(s).wait_send())


class FaceGather:
    def __init__(self, src, out, chips, sems):
        self.src, self.out, self.chips = src, out, chips
        self.send, self.recv, self.fsend, self.frecv = sems
        face = lax.axis_index("face")
        self.face, self.core, self.chip = face, face % 2, face // 2
        self.partner = self.chip * 2 + 1 - self.core

    def direct(self, j):
        return rcopy(
            self.src,
            self.out.at[self.face],
            self.send.at[j],
            self.recv.at[j],
            face=((self.chip + j) % self.chips) * 2 + self.core,
        )

    def forward(self, j):
        block = ((self.chip + self.chips - j) % self.chips) * 2 + self.core
        return rcopy(
            self.src if j == 0 else self.out.at[block],
            self.out.at[block],
            self.fsend.at[j],
            self.frecv.at[j],
            face=self.partner,
        )

    def start(self):
        for j in range(1, self.chips):
            self.direct(j).start()
        self.forward(0).start()

    def relay(self):
        self.relay_first()
        self.relay_rest()

    def relay_first(self):
        pass

    def relay_rest(self):
        for j in range(1, self.chips):
            self.direct(j).wait_recv()
            self.forward(j).start()

    def finish(self):
        for j in range(1, self.chips):
            self.direct(j).wait_send()
        for j in range(self.chips):
            self.forward(j).wait()


class SquareGather:
    def __init__(self, src, out, chips, sems):
        self.src, self.out = src, out
        self.send, self.recv, self.fsend, self.frecv = sems
        face = lax.axis_index("face")
        core, chip = face % 2, face // 2
        col, row = chip % 2, chip // 2
        self.face = face
        self.partner = chip * 2 + 1 - core
        self.beside = (row * 2 + 1 - col) * 2 + core
        self.below = ((1 - row) * 2 + col) * 2 + core
        self.across = ((1 - row) * 2 + 1 - col) * 2 + core
        self.half = src.shape[0] // 2

    def part(self, k):
        return pl.ds((0, 1, 1, 0, 0, 1)[k] * self.half, self.half)

    def came(self, k):
        block = (self.beside, self.beside, self.below, self.below, self.across, self.across)[k]
        return self.out.at[block, self.part(k)]

    def direct(self, k):
        to = (self.beside, self.beside, self.below, self.below, self.below, self.beside)[k]
        if k < 4:
            src, block = self.src.at[self.part(k)], self.face
        else:
            block = self.beside if k == 4 else self.below
            src = self.out.at[block, self.part(k)]
        return rcopy(
            src, self.out.at[block, self.part(k)], self.send.at[k], self.recv.at[k], face=to
        )

    def forward(self, k):
        if k == 6:
            src, dst = self.src, self.out.at[self.face]
        else:
            src = dst = self.came(k)
        return rcopy(src, dst, self.fsend.at[k], self.frecv.at[k], face=self.partner)

    def start(self):
        for k in (0, 2, 1, 3):
            self.direct(k).start()
        self.forward(6).start()

    def relay(self):
        self.relay_first()
        self.relay_rest()

    def relay_first(self):
        for k, onward in ((0, 4), (2, 5)):
            self.direct(k).wait_recv()
            self.direct(onward).start()
            self.forward(k).start()

    def relay_rest(self):
        for k in (1, 3, 4, 5):
            self.direct(k).wait_recv()
            self.forward(k).start()

    def finish(self):
        for k in range(6):
            self.direct(k).wait_send()
        for k in range(7):
            self.forward(k).wait()


def gather_over_face(src, out, chips, sems):
    kind = SquareGather if chips == 4 and src.shape[0] % 2 == 0 else FaceGather
    return kind(src, out, chips, sems)


def dma_sems(*sizes):
    return [pltpu.SemaphoreType.DMA((max(n, 1),)) for n in sizes]


def first_gather_kernel(chips, members, count, *refs):
    x, ws = refs[0], refs[1 : 1 + count]
    edges_out, outs = refs[1 + count], refs[2 + count : 2 + 2 * count]
    edges, field, own_sem = refs[2 + 2 * count : 5 + 2 * count]
    sems = refs[5 + 2 * count :]
    face = lax.axis_index("face")
    member = lax.axis_index("member")
    own = []
    for k in range(count):
        place = outs[k].at[member] if k else outs[k].at[face, member]
        own.append(pltpu.make_async_copy(ws[k], place, own_sem.at[k + 1]))
        own[k].start()

    def cut(k, carry):
        field[...] = x[k].astype(f32)
        sides_out(field, edges, k)
        return carry

    lax.fori_loop(0, x.shape[0], cut, 0)
    greet(chips, members, True, True)
    eg = gather_over_face(edges, edges_out, chips, sems[:4])
    eg.start()
    edges_out[face] = edges[...]
    for c in own:
        c.wait()
    rest = sems[4:]
    line_gather(ws[0], lambda b: outs[0].at[face, b], member, members, rest[:4])
    wg = gather_over_face(outs[0].at[face], outs[0], chips, rest[4:8])
    wg.start()
    eg.relay_first()
    for k in range(1, count):
        line = rest[4 * k + 4 : 4 * k + 8]
        line_gather(ws[k], lambda b: outs[k].at[b], member, members, line)
    eg.relay_rest()
    wg.relay()
    eg.finish()
    wg.finish()


def first_gather(x, ws, faces, members):
    chips = faces // 2
    count = len(ws)
    n, h, w, c = x.shape
    shapes = [jax.ShapeDtypeStruct((faces, n, 4, w, c), x.dtype)] + [
        jax.ShapeDtypeStruct((members,) + v.shape, v.dtype) for v in ws
    ]
    shapes[1] = jax.ShapeDtypeStruct((faces,) + shapes[1].shape, shapes[1].dtype)
    scratch = [VMEM((n, 4, w, c), x.dtype), VMEM((h, w, c), f32)]
    scratch += dma_sems(count + 1) + dma_sems(*([chips + 3] * 4))
    scratch += dma_sems(*([members] * 4)) + dma_sems(*([chips + 3] * 4))
    scratch += dma_sems(*([members] * 4)) * (count - 1)
    return pl.pallas_call(
        functools.partial(first_gather_kernel, chips, members, count),
        out_shape=shapes,
        in_specs=[pl.BlockSpec(memory_space=VMEM)] * (count + 1),
        out_specs=[pl.BlockSpec(memory_space=VMEM)] * (count + 1),
        scratch_shapes=scratch,
        compiler_params=pltpu.CompilerParams(
            collective_id=1, has_side_effects=True, vmem_limit_bytes=LIMIT
        ),
        name="first_gather",
    )(x, *ws)


def face_gather_kernel(chips, x, out, own_sem, *sems):
    own = pltpu.make_async_copy(x, out.at[lax.axis_index("face")], own_sem.at[0])
    own.start()
    greet(chips, 1, True, False)
    g = gather_over_face(x, out, chips, sems)
    g.start()
    own.wait()
    g.relay()
    g.finish()


def face_gather(x, faces, ident):
    chips = faces // 2
    return pl.pallas_call(
        functools.partial(face_gather_kernel, chips),
        out_shape=jax.ShapeDtypeStruct((faces,) + x.shape, x.dtype),
        in_specs=[pl.BlockSpec(memory_space=VMEM)],
        out_specs=pl.BlockSpec(memory_space=VMEM),
        scratch_shapes=dma_sems(1) + dma_sems(*([chips + 3] * 4)),
        compiler_params=pltpu.CompilerParams(
            collective_id=ident, has_side_effects=True, vmem_limit_bytes=LIMIT
        ),
        name="face_gather",
    )(x)


def score_kernel(members, held, tile_dev, chunk, h, *refs):
    y, obs, out, packed, came, slopes, back = refs[:7]
    s1, r1, s2, r2 = refs[7:]
    member = lax.axis_index("member")
    part = obs.shape[-1]
    ensemble = held * members
    chunks = tile_dev // chunk

    def there(j):
        return (member + j) % members

    def source(j):
        return (member + members - j) % members

    def go(i, j):
        at = pl.ds(i * chunk, chunk)
        return rcopy(
            packed.at[there(j), at], came.at[j, at], s1.at[i, j], r1.at[i, j], member=there(j)
        )

    def home(i, j):
        at = pl.ds(i * chunk, chunk)
        return rcopy(
            slopes.at[j, at], back.at[member, at], s2.at[i, j], r2.at[i, j], member=source(j)
        )

    def home_here(i, j):
        at = pl.ds(i * chunk, chunk)
        return rcopy(
            slopes.at[j, at], back.at[there(j), at], s2.at[i, j], r2.at[i, j], member=source(j)
        )

    def pack(t):
        for q in range(members):
            packed[q, t] = jnp.concatenate(
                [y[m * tile_dev + t][:, q * part : (q + 1) * part] for m in range(held)], axis=1
            )

    def g(v):
        return v * lax.rsqrt(v * v + smooth_sq)

    def score(t):
        o = obs[t].astype(f32)
        o = jnp.concatenate([o] * held, axis=1)
        vals = [packed[member, t].astype(f32)]
        vals += [came[j, t].astype(f32) for j in range(1, members)]
        turned = [
            jnp.concatenate([v[:, k * part :], v[:, : k * part]], axis=1) if k else v
            for v in vals
            for k in range(held)
        ]
        for j in range(members):
            v = vals[j]
            paired = jnp.zeros_like(v)
            for u in turned:
                paired = paired + g(v - u)
            s = (g(v - o) / ensemble - paired / (ensemble * ensemble)) / h
            s = s.astype(bf16)
            if j == 0:
                back[member, t] = s
            else:
                slopes[j, t] = s

    pack_first = [pack(t) for t in range(chunk)]
    del pack_first
    greet(1, members, False, True)
    for i in range(chunks):
        if i:
            for t in range(i * chunk, (i + 1) * chunk):
                pack(t)
        for j in range(1, members):
            go(i, j).start()
    for i in range(chunks):
        for j in range(1, members):
            go(i, j).wait_recv()
        for t in range(i * chunk, (i + 1) * chunk):
            score(t)
        for j in range(1, members):
            home(i, j).start()
    for i in range(chunks):
        for j in range(1, members):
            home_here(i, j).wait_recv()
        for t in range(i * chunk, (i + 1) * chunk):
            for m in range(held):
                out[m * tile_dev + t] = jnp.concatenate(
                    [back[q, t][:, m * part : (m + 1) * part] for q in range(members)], axis=1
                )
    for i in range(chunks):
        for j in range(1, members):
            go(i, j).wait_send()
            home(i, j).wait_send()


def score_exchange(y, obs, members, h, ident):
    n, variables, cells = y.shape
    tile_dev = obs.shape[0]
    held = n // tile_dev
    chunk = 2 if tile_dev % 2 == 0 else 1
    wide = (members, tile_dev, variables, held * obs.shape[-1])
    sems = pltpu.SemaphoreType.DMA((tile_dev // chunk, members))
    return pl.pallas_call(
        functools.partial(score_kernel, members, held, tile_dev, chunk, h),
        out_shape=jax.ShapeDtypeStruct(y.shape, bf16),
        in_specs=[pl.BlockSpec(memory_space=VMEM)] * 2,
        out_specs=pl.BlockSpec(memory_space=VMEM),
        scratch_shapes=[VMEM(wide, bf16)] * 4 + [sems] * 4,
        compiler_params=pltpu.CompilerParams(
            collective_id=ident, has_side_effects=True, vmem_limit_bytes=LIMIT
        ),
        name="score",
    )(y, obs)


class Scatter:
    def __init__(self, g, out, chips, members, scratch):
        self.g, self.out, self.chips, self.members = g, out, chips, members
        self.fromcore, self.acc, self.fromchip, self.fromline = scratch[:4]
        self.s0, self.r0, self.s1, self.r1, self.s2, self.r2 = scratch[4:]
        face = lax.axis_index("face")
        self.member = lax.axis_index("member")
        self.core, self.chip = face % 2, face // 2
        self.partner = self.chip * 2 + 1 - self.core
        self.order = list(range(1, chips)) + [0]

    def there(self, j):
        return (self.chip + j) % self.chips

    def core_copy(self, j):
        return rcopy(
            self.g.at[self.there(j), 1 - self.core],
            self.fromcore.at[j],
            self.s0.at[j],
            self.r0.at[j],
            face=self.partner,
        )

    def chip_copy(self, j):
        return rcopy(
            self.acc.at[j],
            self.fromchip.at[j],
            self.s1.at[j],
            self.r1.at[j],
            face=self.there(j) * 2 + self.core,
        )

    def line_copy(self, j):
        to = (self.member + j) % self.members
        return rcopy(
            self.acc.at[0, to], self.fromline.at[j], self.s2.at[j], self.r2.at[j], member=to
        )

    def core_start(self):
        for j in self.order:
            self.core_copy(j).start()

    def core_done(self):
        for j in self.order:
            self.core_copy(j).wait_recv()
            self.acc[j] = self.g[self.there(j), self.core] + self.fromcore[j]
            if j:
                self.chip_copy(j).start()

    def chip_done(self):
        for j in range(1, self.chips):
            self.chip_copy(j).wait_recv()
            self.acc[0] = self.acc[0] + self.fromchip[j]
        for j in range(1, self.members):
            self.line_copy(j).start()

    def line_done(self):
        total = self.acc[0, self.member]
        for j in range(1, self.members):
            self.line_copy(j).wait_recv()
            total = total + self.fromline[j]
        self.out[...] = total

    def finish(self):
        for j in range(self.chips):
            self.core_copy(j).wait_send()
        for j in range(1, self.chips):
            self.chip_copy(j).wait_send()
        for j in range(1, self.members):
            self.line_copy(j).wait_send()


def scatter_scratch(chips, members, tail):
    return [
        VMEM((chips, members) + tail, f32),
        VMEM((chips, members) + tail, f32),
        VMEM((chips, members) + tail, f32),
        VMEM((members,) + tail, f32),
    ] + dma_sems(chips, chips, chips, chips, members, members)


def rims_of(index_ref, flip_ref, edges_ref, n, length):
    cat = jnp.concatenate([edges_ref[index_ref[n * 4 + a]] for a in range(4)], axis=0)
    size = 4 * length
    row = lax.broadcasted_iota(jnp.int32, (size, size), 0)
    col = lax.broadcasted_iota(jnp.int32, (size, size), 1)
    side = row // length
    place = row - side * length
    flag = jnp.zeros((size, size), jnp.int32)
    for a in range(4):
        flag = jnp.where(side == a, flip_ref[n * 4 + a], flag)
    target = side * length + jnp.where(flag == 1, length - 1 - place, place)
    return mm(jnp.where(col == target, 1.0, 0.0).astype(bf16), cat)


def col_to_rows(ref_slice):
    height, _, channels = ref_slice.shape
    return ref_slice.reshape(height, channels)


def sides_out(field, edge_ref, k):
    w = field.shape[1]
    h = field.shape[0]
    edge_ref[k, 0] = field[0].astype(bf16)
    edge_ref[k, 1] = col_to_rows(field[:, w - 1 : w, :]).astype(bf16)
    edge_ref[k, 2] = field[h - 1].astype(bf16)
    edge_ref[k, 3] = col_to_rows(field[:, 0:1, :]).astype(bf16)


def silu(v):
    return v / (1.0 + jnp.exp(-v))


def dsilu(v):
    s = 1.0 / (1.0 + jnp.exp(-v))
    return s * (1.0 + v * (1.0 - s))


def table_kernel(members, tile_dev, place_ref, glue_ref, index_ref, flip_ref, slot_of):
    first = lax.axis_index("face") * tile_dev

    def invert(s, carry):
        slot_of[place_ref[s]] = s
        return carry

    lax.fori_loop(0, place_ref.shape[0], invert, 0)

    def fill(i, carry):
        tile = place_ref[first + i]
        for a in range(4):
            base = (tile * 4 + a) * 3
            slot = slot_of[glue_ref[base]]
            face = slot // tile_dev
            inner = slot - face * tile_dev
            for m in range(members):
                at = (m * tile_dev + i) * 4 + a
                index_ref[at] = ((face * members + m) * tile_dev + inner) * 4 + glue_ref[base + 1]
                flip_ref[at] = glue_ref[base + 2]
        return carry

    lax.fori_loop(0, tile_dev, fill, 0)


def edge_table(placement_map, glue, members, tile_dev):
    size = members * tile_dev * 4
    return pl.pallas_call(
        functools.partial(table_kernel, members, tile_dev),
        out_shape=[jax.ShapeDtypeStruct((size,), jnp.int32)] * 2,
        in_specs=[SMEM_SPEC] * 2,
        out_specs=[SMEM_SPEC] * 2,
        scratch_shapes=[pltpu.SMEM(placement_map.shape, jnp.int32)],
        name="table",
    )(placement_map, glue)


def conv_kernel(block, steps, chips, *refs):
    last = chips is None
    index_ref, flip_ref, x_ref, edges_ref, w_ref = refs[:5]
    if last:
        head_ref, x3_ref, pre_ref, act_ref, out_ref, pad = refs[5:]
    else:
        late, late_out = refs[5:7], refs[11:13]
        x3_ref, pre_ref, act_ref, side_ref = refs[7:11]
        pad, field, own_sem = refs[13:16]
        gathers = [
            gather_over_face(late[k], late_out[k], chips, refs[16 + 4 * k : 20 + 4 * k])
            for k in range(2)
        ]
        own = [
            pltpu.make_async_copy(
                late[k], late_out[k].at[lax.axis_index("face")], own_sem.at[k]
            )
            for k in range(2)
        ]
    _, h, w, c = x_ref.shape
    step = pl.program_id(0)
    if not last:

        @pl.when(step == 0)
        def _():
            for copy in own:
                copy.start()
            greet(chips, 1, True, False)
            for gather in gathers:
                gather.start()

    for k in range(block):
        n = step * block + k
        rims = rims_of(index_ref, flip_ref, edges_ref, n, w)
        zero = jnp.zeros((8, c), f32)
        for r in (0, h + 1):
            pad[r, 0:8, :] = zero
            pad[r, 8 + w : 16 + w, :] = zero
        pad[1 : h + 1, 8 : 8 + w, :] = x_ref[k].astype(f32)
        pad[0, 8 : 8 + w, :] = rims[0:w]
        pad[1 : h + 1, 8 + w : 9 + w, :] = rims[w : w + h].reshape(h, 1, c)
        pad[h + 1, 8 : 8 + w, :] = rims[w + h : 2 * w + h]
        pad[1 : h + 1, 7:8, :] = rims[2 * w + h :].reshape(h, 1, c)
        for b in range(3):
            x3_ref[k, :, :, b * c : (b + 1) * c] = pad[:, 7 + b : 7 + b + w, :].astype(bf16)
    pre = None
    for a in range(3):
        part = mm(
            x3_ref[:, a : a + h].reshape(block * h * w, 3 * c),
            w_ref[3 * a * c : 3 * (a + 1) * c, :],
        )
        pre = part if pre is None else pre + part
    pre_ref[...] = pre.reshape(block, h * w, c)
    act = silu(pre).astype(bf16)
    act_ref[...] = act.reshape(act_ref.shape)
    if last:
        for k in range(block):
            out_ref[k] = mm(head_ref[...], act[k * h * w : (k + 1) * h * w], NT).astype(bf16)
    else:
        for k in range(block):
            field[...] = act[k * h * w : (k + 1) * h * w].astype(f32).reshape(h, w, c)
            sides_out(field, side_ref, k)

        @pl.when(step == min(1, steps - 1))
        def _():
            for gather in gathers:
                gather.relay_first()

        @pl.when(step == steps - 1)
        def _():
            for gather in gathers:
                gather.relay_rest()
            for copy in own:
                copy.wait()
            for gather in gathers:
                gather.finish()


def whole(shape):
    return pl.BlockSpec(shape, lambda i: (0,) * len(shape))


def tiles(block, shape):
    return pl.BlockSpec((block,) + shape, lambda i: (i,) + (0,) * len(shape))


SMEM_SPEC = pl.BlockSpec(memory_space=pltpu.SMEM)


def block_of(n):
    return 3 if n % 3 == 0 else (2 if n % 2 == 0 else 1)


def conv(scalars, x, edges, w, faces=None, late=None, head_t=None):
    n, h, wd, c = x.shape
    block = block_of(n)
    last = head_t is not None
    chips = None if last else faces // 2
    in_specs = [
        SMEM_SPEC,
        SMEM_SPEC,
        tiles(block, (h, wd, c)),
        whole(edges.shape),
        whole(w.shape),
    ]
    shapes = [
        jax.ShapeDtypeStruct((n, h + 2, wd, 3 * c), bf16),
        jax.ShapeDtypeStruct((n, h * wd, c), f32),
        jax.ShapeDtypeStruct((n, h * wd, c) if last else (n, h, wd, c), bf16),
    ]
    args = [*scalars, x, edges, w]
    scratch = [VMEM((h + 2, wd + 16, c), f32)]
    extra = {}
    if last:
        in_specs.append(whole(head_t.shape))
        args.append(head_t)
        shapes.append(jax.ShapeDtypeStruct((n, head_t.shape[0], h * wd), bf16))
    else:
        in_specs += [whole(v.shape) for v in late]
        args += late
        shapes.append(jax.ShapeDtypeStruct((n, 4, wd, c), bf16))
        scratch.append(VMEM((h, wd, c), f32))
        scratch += dma_sems(2) + dma_sems(*([chips + 3] * 8))
        extra = dict(collective_id=6, has_side_effects=True)
    out_specs = [tiles(block, s.shape[1:]) for s in shapes]
    if not last:
        shapes += [jax.ShapeDtypeStruct((faces,) + v.shape, v.dtype) for v in late]
        out_specs += [pl.BlockSpec(memory_space=pl.ANY)] * 2
    return pl.pallas_call(
        functools.partial(conv_kernel, block, n // block, chips),
        grid=(n // block,),
        out_shape=shapes,
        in_specs=in_specs,
        out_specs=out_specs,
        scratch_shapes=scratch,
        compiler_params=pltpu.CompilerParams(vmem_limit_bytes=LIMIT, **extra),
        name="conv_last" if last else "conv_first",
    )(*args)


def back_kernel(block, h, w, *refs):
    out_ref, act_ref, pre_ref, head_ref, w_ref = refs[:5]
    slope_ref, inner_ref, side_ref, hg_ref, va, vb, pad, s3, cols = refs[5:]
    c = act_ref.shape[-1]
    step = pl.program_id(0)

    @pl.when(step == 0)
    def _():
        hg_ref[...] = jnp.zeros_like(hg_ref)
        for a in range(3):
            for b in range(3):
                tap = w_ref[(3 * a + b) * c : (3 * a + b + 1) * c, :]
                va[a, :, b * c : (b + 1) * c] = tap
                if b == 0:
                    vb[0, :, a * c : (a + 1) * c] = tap
                if b == 2:
                    vb[1, :, a * c : (a + 1) * c] = tap
        pad[...] = jnp.zeros_like(pad)

    for k in range(block):
        slope_out = out_ref[k]
        hg_ref[...] += mm(slope_out, act_ref[k])
        back = mm(slope_out, head_ref[...], TN)
        slope = (back * dsilu(pre_ref[k])).astype(bf16)
        slope_ref[k] = slope
        pad[2 : h + 2, 8 : 8 + w, :] = slope.astype(f32).reshape(h, w, c)
        for b in range(3):
            s3[k, :, :, b * c : (b + 1) * c] = pad[:, 9 - b : 9 - b + w, :].astype(bf16)
        left = pad[:, 8:9, :].reshape(h + 4, c)
        right = pad[:, 7 + w : 8 + w, :].reshape(h + 4, c)
        for a in range(3):
            cols[0, k, :, a * c : (a + 1) * c] = left[3 - a : 3 - a + h].astype(bf16)
            cols[1, k, :, a * c : (a + 1) * c] = right[3 - a : 3 - a + h].astype(bf16)
    full = None
    for a in range(3):
        part = mm(s3[:, 2 - a : 20 - a + h - 16].reshape(block * (h + 2) * w, 3 * c), va[a], NT)
        full = part if full is None else full + part
    full = full.reshape(block, h + 2, w, c).astype(bf16)
    inner_ref[...] = full[:, 1 : h + 1]
    lefts = mm(cols[0].reshape(block * h, 3 * c), vb[0], NT).astype(bf16)
    rights = mm(cols[1].reshape(block * h, 3 * c), vb[1], NT).astype(bf16)
    for k in range(block):
        side_ref[k, 0] = full[k, 0]
        side_ref[k, 1] = rights[k * h : (k + 1) * h]
        side_ref[k, 2] = full[k, h + 1]
        side_ref[k, 3] = lefts[k * h : (k + 1) * h]


def backward(slope_out, act, pre, head_t, w, h, wd):
    n, cells, c = act.shape
    block = block_of(n)
    shapes = [
        jax.ShapeDtypeStruct((n, cells, c), bf16),
        jax.ShapeDtypeStruct((n, h, wd, c), bf16),
        jax.ShapeDtypeStruct((n, 4, wd, c), bf16),
        jax.ShapeDtypeStruct(head_t.shape, f32),
    ]
    return pl.pallas_call(
        functools.partial(back_kernel, block, h, wd),
        grid=(n // block,),
        out_shape=shapes,
        in_specs=[
            tiles(block, slope_out.shape[1:]),
            tiles(block, (cells, c)),
            tiles(block, (cells, c)),
            whole(head_t.shape),
            whole(w.shape),
        ],
        out_specs=[tiles(block, s.shape[1:]) for s in shapes[:3]] + [whole(head_t.shape)],
        scratch_shapes=[
            VMEM((3, c, 3 * c), bf16),
            VMEM((2, c, 3 * c), bf16),
            VMEM((h + 4, wd + 16, c), f32),
            VMEM((block, h + 4, wd, 3 * c), bf16),
            VMEM((2, block, h, 3 * c), bf16),
        ],
        compiler_params=pltpu.CompilerParams(vmem_limit_bytes=LIMIT),
        name="backward",
    )(slope_out, act, pre, head_t, w)


def add_products(acc, slopes, x3_ref, h, w):
    block, _, _, width = x3_ref.shape
    turned = jnp.concatenate([v.T for v in slopes], axis=1)
    for a in range(3):
        acc[a] += mm(turned, x3_ref[:, a : a + h].reshape(block * h * w, width))


def turn_out(acc, out_ref):
    c = out_ref.shape[-1]
    for a in range(3):
        for b in range(3):
            out_ref[(3 * a + b) * c : (3 * a + b + 1) * c, :] = acc[
                a, :, b * c : (b + 1) * c
            ].T


def grad_two_kernel(block, steps, chips, h, w, *refs):
    slope_ref, x3_ref, side_ref, out_ref, sides_ref, acc, own_sem = refs[:7]
    step = pl.program_id(0)
    gather = gather_over_face(side_ref, sides_ref, chips, refs[7:])
    own = pltpu.make_async_copy(side_ref, sides_ref.at[lax.axis_index("face")], own_sem.at[0])

    @pl.when(step == 0)
    def _():
        own.start()
        greet(chips, 1, True, False)
        gather.start()
        acc[...] = jnp.zeros_like(acc)

    add_products(acc, [slope_ref[k] for k in range(block)], x3_ref, h, w)

    @pl.when(step == min(1, steps - 1))
    def _():
        gather.relay_first()

    @pl.when(step == steps - 1)
    def _():
        turn_out(acc, out_ref)
        own.wait()
        gather.relay_rest()
        gather.finish()


def grad_two_gather(x3, slope, sides, h, w, faces, ident):
    n, _, _, width = x3.shape
    c = width // 3
    block = block_of(n)
    chips = faces // 2
    return pl.pallas_call(
        functools.partial(grad_two_kernel, block, n // block, chips, h, w),
        grid=(n // block,),
        out_shape=[
            jax.ShapeDtypeStruct((9 * c, c), f32),
            jax.ShapeDtypeStruct((faces,) + sides.shape, sides.dtype),
        ],
        in_specs=[
            tiles(block, slope.shape[1:]),
            tiles(block, x3.shape[1:]),
            whole(sides.shape),
        ],
        out_specs=[whole((9 * c, c)), pl.BlockSpec(memory_space=pl.ANY)],
        scratch_shapes=[VMEM((3, c, width), f32)]
        + dma_sems(1)
        + dma_sems(*([chips + 3] * 4)),
        compiler_params=pltpu.CompilerParams(
            collective_id=ident, has_side_effects=True, vmem_limit_bytes=LIMIT
        ),
        name="grad_two",
    )(slope, x3, sides)


def grad_one_kernel(block, steps, chips, members, h, w, *refs):
    index_ref, flip_ref, edges_ref, inner_ref, pre_ref, x3_ref, two_ref, hg_ref = refs[:8]
    one_out, two_out, hg_out, acc, field, one_flat, one = refs[8:15]
    rest = refs[15:]
    c = one_flat.shape[-1]
    step = pl.program_id(0)
    s_two = Scatter(two_ref, two_out, chips, members, rest[:10])
    s_head = Scatter(hg_ref, hg_out, chips, members, rest[10:20])
    s_one = Scatter(one, one_out, chips, members, rest[20:30])

    @pl.when(step == 0)
    def _():
        greet(chips, members, True, True)
        s_two.core_start()
        s_head.core_start()
        acc[...] = jnp.zeros_like(acc)

    slopes = []
    for k in range(block):
        rims = rims_of(index_ref, flip_ref, edges_ref, step * block + k, w)
        field[...] = inner_ref[k].astype(f32)
        field[0] += rims[0:w]
        field[:, w - 1 : w, :] += rims[w : w + h].reshape(h, 1, c)
        field[h - 1] += rims[w + h : 2 * w + h]
        field[:, 0:1, :] += rims[2 * w + h :].reshape(h, 1, c)
        slopes.append((field[...].reshape(h * w, c) * dsilu(pre_ref[k])).astype(bf16))
    add_products(acc, slopes, x3_ref, h, w)

    @pl.when(step == 0)
    def _():
        s_two.core_done()
        s_head.core_done()

    @pl.when(step == steps - 1)
    def _():
        turn_out(acc, one_flat)
        rows = one.shape[3]
        for d in range(chips * 2 * members):
            one[d // (2 * members), d // members % 2, d % members] = one_flat[
                d * rows : (d + 1) * rows
            ]
        s_one.core_start()
        s_one.core_done()
        s_two.chip_done()
        s_head.chip_done()
        s_one.chip_done()
        s_two.line_done()
        s_head.line_done()
        s_one.line_done()
        for s in (s_two, s_head, s_one):
            s.finish()


def grad_one_scatter(scalars, edges, inner, pre, x3, two, hg, faces, members, ident):
    n, h, w, c = inner.shape
    block = block_of(n)
    chips = faces // 2
    tails = [two.shape[3:], hg.shape[3:], two.shape[3:]]
    scratch = [
        VMEM((3, c, 3 * c), f32),
        VMEM((h, w, c), f32),
        VMEM((9 * c, c), f32),
        VMEM(two.shape, f32),
    ]
    for tail in tails:
        scratch += scatter_scratch(chips, members, tail)
    return pl.pallas_call(
        functools.partial(grad_one_kernel, block, n // block, chips, members, h, w),
        grid=(n // block,),
        out_shape=[jax.ShapeDtypeStruct(tails[k], f32) for k in (2, 0, 1)],
        in_specs=[
            SMEM_SPEC,
            SMEM_SPEC,
            whole(edges.shape),
            tiles(block, inner.shape[1:]),
            tiles(block, pre.shape[1:]),
            tiles(block, x3.shape[1:]),
            whole(two.shape),
            whole(hg.shape),
        ],
        out_specs=[whole(tails[k]) for k in (2, 0, 1)],
        scratch_shapes=scratch,
        compiler_params=pltpu.CompilerParams(
            collective_id=ident, has_side_effects=True, vmem_limit_bytes=LIMIT
        ),
        name="grad_one",
    )(*scalars, edges, inner, pre, x3, two, hg)


def shards(faces, zs, features, observed, conv_weights, head_weight, adjacency, placement_map):
    members, tile_dev, h, w, c = features.shape
    n = members * tile_dev
    variables = head_weight.shape[1]
    x = features.reshape(n, h, w, c)
    rows = conv_weights.shape[0]
    head_rows = head_weight.shape[0]
    lanes = -(-variables // 128) * 128
    head_wide = jnp.pad(head_weight, ((0, 0), (0, lanes - variables)))
    edges, w0, w1_line, head_line = first_gather(
        x, [conv_weights[:, 0], conv_weights[:, 1], head_wide], faces, zs
    )
    w0 = w0.reshape(faces * zs * rows, c)

    def flat(e):
        return e.reshape((faces * n * 4,) + e.shape[-2:])

    scalars = edge_table(placement_map, adjacency.reshape(-1), members, tile_dev)
    index, flips = scalars
    x3_one, pre_one, act_one, sides, w1, head = conv(
        scalars, x, flat(edges), w0, faces=faces, late=[w1_line, head_line]
    )
    w1 = w1.reshape(faces * zs * rows, c)
    head_t = head.reshape(faces * zs * head_rows, lanes)[:, :variables].T
    x3_two, pre_two, act_two, outs = conv(
        scalars, act_one, flat(face_gather(sides, faces, 2)), w1, head_t=head_t
    )
    slope_out = score_exchange(outs, observed, zs, h, 3)
    slope_two, inner, borders, hg = backward(slope_out, act_two, pre_two, head_t, w1, h, w)
    grad_two, returned = grad_two_gather(x3_two, slope_two, borders, h, w, faces, 4)
    hg = jnp.pad(hg.T, ((0, 0), (0, lanes - variables)))
    chips = faces // 2
    one, two, head_out = grad_one_scatter(
        (index, flips),
        flat(returned),
        inner,
        pre_one,
        x3_one,
        grad_two.reshape(chips, 2, zs, rows, c),
        hg.reshape(chips, 2, zs, head_rows, lanes),
        faces,
        zs,
        5,
    )
    return jnp.stack([one, two], axis=1), head_out[:, :variables]


def solution(mesh):
    in_specs = (
        P("member", "face", None, None, None),
        P("face", None, "member"),
        P(("face", "member"), None, None),
        P(("face", "member"), None),
        P(),
        P(),
    )
    out_specs = (P(("face", "member"), None, None), P(("face", "member"), None))
    body = functools.partial(shards, mesh.shape["face"], mesh.shape["member"])
    return jax.shard_map(body, mesh=mesh, in_specs=in_specs, out_specs=out_specs, check_vma=False)
```
